32 devices in a mesh: dp: 4 (over z), seq: 8 (over y, x, core).
Axes of the slice: x: 2, y: 2, z: 4, core: 2. Of those that a mesh axis runs over, the one named last changes fastest.
Arguments:
- layer_input: bfloat16 [4, 2048, 1024], P('dp', 'seq'), may hold values from -6 to 6
- w_qkv: bfloat16 [1024, 3072], replicated, may hold values from -8.75 to 8.75
- w_out: bfloat16 [1024, 1024], replicated, may hold values from -0.1875 to 0.1875
- w_proj: bfloat16 [16, 64, 256], replicated, may hold values from -35 to 35
- w_up: bfloat16 [1024, 4096], P('dp', 'seq'), may hold values from -0.1875 to 0.1875
- w_down: bfloat16 [1024, 4096], P('dp', 'seq'), may hold values from -0.09375 to 0.09375
Outputs:
- layer_output: bfloat16 [4, 2048, 1024], P('dp', 'seq')
The draws below stay inside these ranges and needn't reach their ends.
All inputs are finite; a program needn't handle non-finite values.
Results may differ from the reference program's by a relative error of at most 0.025.
The reference program's roundings to bfloat16 on the way count: a program that leaves them out, or rounds other values in their place, can miss the bound.
Values may be sent and summed in bfloat16 or wider, within the bound.
No kernel may reach another device: no remote copies, remote signals or barrier semaphores. Data moves between devices by JAX's collectives and lax.ppermute only.
A program may use at most 128 MiB of HBM per device.

```python
import jax
import jax.numpy as jnp
from jax import lax

D = 1024
H = 16
HS = 64
R = 256
FF = 4096
WBLK = 256
SEQS = 4
LENGTH = 2048


def draw_w_qkv(key, part):
    base = jnp.clip(jax.random.normal(jax.random.fold_in(key, 11), (D, 3 * D), jnp.float32), -4.0, 4.0) * D ** (-0.5)
    return base.astype(jnp.bfloat16)


def draw_w_proj(key, part):
    base = jnp.clip(jax.random.normal(jax.random.fold_in(key, 21), (H, HS, R), jnp.float32), -4.0, 4.0) * HS ** (-0.5)
    return base.astype(jnp.bfloat16)


def shard_levels(stream_key, dims, shards, smallest, top_value):
    factor_of = 1.0
    for position, blocks in shards:
        heights = jax.random.uniform(jax.random.fold_in(jax.random.fold_in(stream_key, 6), position), (blocks,), jnp.float32, smallest / len(shards), top_value / len(shards))
        factor_of = factor_of * jnp.repeat(jnp.exp(heights), dims[position] // blocks).reshape((-1,) + (1,) * (len(dims) - 1 - position))
    return factor_of


def scatter_about(stream_key, shape, width, limit, cuts=(), held_as=jnp.bfloat16):
    values = jax.random.normal(stream_key, shape, jnp.float32) * width
    if len(cuts) > 0:
        values = shard_levels(stream_key, shape, cuts, -0.22, 0.18) * values
    return jnp.clip(values, min=-limit, max=limit).astype(held_as)


def setup_inputs(seed: int = 0) -> dict:
    streams_of = jax.random.split(jax.random.key(seed), 7)
    return {
        "layer_input": scatter_about(streams_of[0], (SEQS, LENGTH, D), 1.0, 6.0, ((0, 4), (1, 8))),
        "w_qkv": draw_w_qkv(jax.random.fold_in(streams_of[6], 71), 0),
        "w_out": scatter_about(streams_of[2], (D, D), D ** -0.5, 0.1875),
        "w_proj": draw_w_proj(jax.random.fold_in(streams_of[6], 71), 0),
        "w_up": scatter_about(streams_of[4], (D, FF), D ** -0.5, 0.1875, ((0, 4), (1, 8))),
        "w_down": scatter_about(streams_of[5], (D, FF), FF ** -0.5, 0.09375, ((0, 4), (1, 8))),
    }


epsilon = 1e-05

def normalize(value):
    center = value - lax.optimization_barrier(jnp.mean(value, axis=-1, keepdims=True))
    spread = lax.optimization_barrier(jnp.mean(center * center, axis=-1, keepdims=True))
    return center * lax.rsqrt(spread + epsilon)

def attend(block_query, near_keys, near_values, inside, far_keys, far_values):
    scale = HS ** (-0.5)
    query_wide = block_query.astype(jnp.float32)
    near = jnp.einsum('qhd,khd->hqk', query_wide, near_keys.astype(jnp.float32)) * scale
    near = jnp.where(inside[None, None, :], near, -jnp.inf)
    far = jnp.einsum('qhd,hrd->hqr', query_wide, far_keys.astype(jnp.float32)) * scale
    weights = jax.nn.softmax(jnp.concatenate([near, far], axis=-1), axis=-1).astype(jnp.bfloat16)
    weights = lax.optimization_barrier(weights).astype(jnp.float32)
    reach = near_keys.shape[0]
    mixed = jnp.einsum('hqk,khd->qhd', weights[..., :reach], near_values.astype(jnp.float32))
    mixed = mixed + jnp.einsum('hqr,hrd->qhd', weights[..., reach:], far_values.astype(jnp.float32))
    return mixed.astype(jnp.bfloat16).reshape(block_query.shape[0], H * HS)

def one_sequence(tokens, w_qkv, w_out, w_proj, w_up, w_down):
    length = tokens.shape[0]
    normed = normalize(tokens.astype(jnp.float32)).astype(jnp.bfloat16)
    qkv = jnp.dot(normed, w_qkv, preferred_element_type=jnp.float32).astype(jnp.bfloat16)
    query = qkv[:, :D].reshape(length, H, HS)
    keys = qkv[:, D:2 * D].reshape(length, H, HS)
    values = qkv[:, 2 * D:].reshape(length, H, HS)
    logits = jnp.einsum('nhd,hdr->nhr', keys.astype(jnp.float32), w_proj.astype(jnp.float32))
    proj = jax.nn.softmax(logits, axis=0)
    paired = jnp.concatenate([keys, values], axis=-1).astype(jnp.float32)
    summary = jnp.einsum('nhr,nhc->hrc', proj, paired, precision=lax.Precision.HIGHEST)
    far_keys = normalize(summary[..., :HS]).astype(jnp.bfloat16)
    far_values = normalize(summary[..., HS:]).astype(jnp.bfloat16)
    near_keys = normalize(keys.astype(jnp.float32)).astype(jnp.bfloat16)
    near_values = normalize(values.astype(jnp.float32)).astype(jnp.bfloat16)
    padding = ((WBLK, WBLK), (0, 0), (0, 0))
    keys_padded = jnp.pad(near_keys, padding)
    values_padded = jnp.pad(near_values, padding)
    offsets = jnp.arange(3 * WBLK, dtype=jnp.int32) - WBLK

    def per_block(which):
        start = (which * WBLK).astype(jnp.int32)
        block_query = lax.dynamic_slice_in_dim(query, start, WBLK, 0)
        block_keys = lax.dynamic_slice_in_dim(keys_padded, start, 3 * WBLK, 0)
        block_values = lax.dynamic_slice_in_dim(values_padded, start, 3 * WBLK, 0)
        places = start + offsets
        inside = (places >= 0) & (places < length)
        return attend(block_query, block_keys, block_values, inside, far_keys, far_values)
    attn = lax.map(per_block, jnp.arange(length // WBLK, dtype=jnp.int32)).reshape(length, D)
    mixed = (tokens.astype(jnp.float32) + jnp.dot(attn, w_out, preferred_element_type=jnp.float32)).astype(jnp.bfloat16)
    normed_two = normalize(mixed.astype(jnp.float32)).astype(jnp.bfloat16)
    hidden = jax.nn.gelu(jnp.dot(normed_two, w_up, preferred_element_type=jnp.float32)).astype(jnp.bfloat16)
    down = lax.dot_general(hidden, w_down, (((1,), (1,)), ((), ())), preferred_element_type=jnp.float32)
    return (mixed.astype(jnp.float32) + down).astype(jnp.bfloat16)

def reference(layer_input, w_qkv, w_out, w_proj, w_up, w_down):

    def run_one(tokens):
        return one_sequence(tokens, w_qkv, w_out, w_proj, w_up, w_down)
    return lax.map(run_one, layer_input)
```

```python
import functools

import jax
import jax.numpy as jnp
from jax import lax
from jax.experimental import pallas as pl
from jax.experimental.pallas import tpu as pltpu
from jax.sharding import PartitionSpec as P

HS = 64
WBLK = 256
EPS = 1e-05
F32 = jnp.float32
BF = jnp.bfloat16
NT = (((1,), (1,)), ((), ()))
TT = (((0,), (1,)), ((), ()))
VMEM_LIMIT = 60 * 1024 * 1024


def dot(a, b):
    return jnp.dot(a, b, preferred_element_type=F32)


def layer_norm(x):
    center = x - jnp.mean(x, axis=-1, keepdims=True)
    spread = jnp.mean(center * center, axis=-1, keepdims=True)
    return center * lax.rsqrt(spread + EPS)


def head_average(width):
    a = lax.broadcasted_iota(jnp.int32, (width, width), 0) // HS
    b = lax.broadcasted_iota(jnp.int32, (width, width), 1) // HS
    return jnp.where(a == b, 1.0 / HS, 0.0).astype(F32)


def split(x):
    high = x.astype(BF)
    return high, (x - high.astype(F32)).astype(BF)


def head_norm(x):
    avg = head_average(x.shape[1]).astype(BF)
    center = x.astype(F32) - dot(x, avg)
    high, low = split(center * center)
    spread = dot(high, avg) + dot(low, avg)
    return (center * lax.rsqrt(spread + EPS)).astype(BF)


def head_norm_wide(x):
    avg = head_average(x.shape[1]).astype(BF)

    def mean(y):
        one = y.astype(BF)
        rest = y - one.astype(F32)
        two, three = split(rest)
        return dot(one, avg) + dot(two, avg) + dot(three, avg)

    center = x - mean(x)
    spread = mean(center * center)
    return (center * lax.rsqrt(spread + EPS)).astype(BF)


def lanes(shape):
    return lax.broadcasted_iota(jnp.int32, shape, len(shape) - 1)


def diagonal(size):
    return lax.broadcasted_iota(jnp.int32, (size, size), 0) == lax.broadcasted_iota(
        jnp.int32, (size, size), 1
    )


def to_row(column):
    size = column.shape[0]
    return jnp.sum(jnp.where(diagonal(size), column, 0.0), axis=0, keepdims=True)


def to_column(row):
    size = row.shape[1]
    return jnp.sum(jnp.where(diagonal(size), row, 0.0), axis=1, keepdims=True)


def qkv_kernel(sizes, s_ref, tok_ref, par_ref, wq_ref, wk_ref, wv_ref, wp_ref, q_ref, nk_ref, nv_ref, *rest):
    chips, owned, extra, steps, rank = sizes
    pays, (xn_ref, pay_ref, sem) = rest[:chips], rest[chips:]
    rows = tok_ref.shape[0]
    step = pl.program_id(0)

    @pl.when(step == 0)
    def _():
        xn_ref[:rows] = layer_norm(tok_ref[...].astype(F32)).astype(BF)
        xn_ref[rows:] = layer_norm(par_ref[...].astype(F32)).astype(BF)

    x = xn_ref[...]
    kk = dot(x, wk_ref[...]).astype(BF)
    vv = dot(x, wv_ref[...]).astype(BF)
    width = kk.shape[1]
    heads = width // HS
    owners = heads * rank // owned
    stat_rows = owned // 128
    stats = [jnp.zeros((extra, 128), F32) for _ in range(owners)]
    place = lax.broadcasted_iota(jnp.int32, (extra, 128), 0)
    for pair in range(heads // 2):
        kp = kk[:, pair * 128 : (pair + 1) * 128]
        vp = vv[:, pair * 128 : (pair + 1) * 128]
        turned = pltpu.roll(vp.astype(F32), 64, 1).astype(BF)
        low_half = lanes(kp.shape) < HS
        for side in range(2):
            head = pair * 2 + side
            mixed = jnp.where(low_half, kp, turned) if side == 0 else jnp.where(low_half, turned, kp)
            wp = wp_ref[head]
            none = jnp.zeros_like(wp)
            wide = jnp.concatenate([wp, none] if side == 0 else [none, wp], axis=0)
            logits = lax.dot_general(wide, kp, TT, preferred_element_type=F32)
            peak = jnp.max(logits, axis=1, keepdims=True)
            weight = jnp.exp(logits - peak)
            total = jnp.sum(weight, axis=1, keepdims=True)
            high, low = split(weight)
            sums = (dot(high, mixed) + dot(low, mixed)).astype(BF)
            for part in range(rank // 128):
                column = head * rank + part * 128
                owner, offset = column // owned, column % owned
                cut = slice(part * 128, (part + 1) * 128)
                pay_ref[step * owners + owner, offset : offset + 128, :] = sums[cut]
                one = to_row(peak[cut])
                first = one.astype(BF).astype(F32)
                second = (one - first).astype(BF).astype(F32)
                third = one - first - second
                for i, row in enumerate((first, second, third, to_row(total[cut]))):
                    stats[owner] = jnp.where(place == i * stat_rows + offset // 128, row, stats[owner])
    for owner in range(owners):
        pay_ref[step * owners + owner, owned : owned + extra, :] = stats[owner].astype(BF)
    nk_ref[...] = head_norm(kk)
    nv_ref[...] = head_norm(vv)
    q_ref[...] = (dot(x, wq_ref[...]).astype(BF).astype(F32) * HS ** (-0.5)).astype(BF)

    @pl.when(step == steps - 1)
    def _():
        chip = s_ref[1]
        copies = [
            pltpu.make_async_copy(pay_ref.at[lax.bitwise_xor(chip, k)], pays[k], sem.at[k]) for k in range(chips)
        ]
        for copy in copies:
            copy.start()
        for copy in copies:
            copy.wait()


def combine_kernel(sizes, *refs):
    chips, owned, extra = sizes
    pays, far_ref = refs[:chips], refs[chips]
    stat_rows = owned // 128
    tails = [p[owned : owned + extra, :].astype(F32) for p in pays]
    peaks = [
        t[:stat_rows] + t[stat_rows : 2 * stat_rows] + t[2 * stat_rows : 3 * stat_rows] for t in tails
    ]
    peak = functools.reduce(jnp.maximum, peaks)
    scales = [jnp.exp(p - peak) for p in peaks]
    total = sum(s * t[3 * stat_rows : 4 * stat_rows] for s, t in zip(scales, tails))
    scales = [s / total for s in scales]
    for i in range(stat_rows):
        cut = slice(i * 128, (i + 1) * 128)
        summary = sum(to_column(s[i : i + 1]) * p[cut, :].astype(F32) for s, p in zip(scales, pays))
        far_ref[cut, :] = head_norm_wide(summary)


def near_kernel(s_ref, q_ref, nk_ref, nv_ref, halo_ref, halop_ref, wk_ref, wv_ref, o_ref, m_ref, l_ref, xh_ref):
    rows = halo_ref.shape[0]
    step = pl.program_id(0)

    @pl.when(step == 0)
    def _():
        xh_ref[:rows] = layer_norm(halo_ref[...].astype(F32)).astype(BF)
        xh_ref[rows:] = layer_norm(halop_ref[...].astype(F32)).astype(BF)
        m_ref[...] = jnp.zeros_like(m_ref)
        l_ref[...] = jnp.zeros_like(l_ref)

    x = xh_ref[...]
    far_k = head_norm(dot(x, wk_ref[...]).astype(BF))
    far_v = head_norm(dot(x, wv_ref[...]).astype(BF))
    bias = [jnp.where(s_ref[i] > 0, 0.0, -jnp.inf).astype(F32) for i in (2, 3)]
    heads = far_k.shape[1] // HS
    place = lanes(m_ref.shape)
    for pair in range(heads // 2):
        cut = slice(pair * 128, (pair + 1) * 128)
        qp, kp, vp = q_ref[:, cut], nk_ref[:, cut], nv_ref[:, cut]
        hk, hv = far_k[:, cut], far_v[:, cut]
        low_half = lanes(qp.shape) < HS
        outs = []
        for side in range(2):
            none = jnp.zeros_like(qp)
            qm = jnp.where(low_half, qp, none) if side == 0 else jnp.where(low_half, none, qp)
            main = lax.dot_general(qm, kp, NT, preferred_element_type=F32)
            halo = jnp.concatenate(
                [
                    lax.dot_general(qm[:rows], hk[:rows], NT, preferred_element_type=F32) + bias[0],
                    lax.dot_general(qm[rows:], hk[rows:], NT, preferred_element_type=F32) + bias[1],
                ],
                axis=0,
            )
            peak = jnp.maximum(jnp.max(main, axis=1, keepdims=True), jnp.max(halo, axis=1, keepdims=True))
            main = jnp.exp(main - peak)
            halo = jnp.exp(halo - peak)
            total = jnp.sum(main, axis=1, keepdims=True) + jnp.sum(halo, axis=1, keepdims=True)
            halo = halo.astype(BF)
            out = dot(main.astype(BF), vp) + jnp.concatenate(
                [dot(halo[:rows], hv[:rows]), dot(halo[rows:], hv[rows:])], axis=0
            )
            outs.append(out)
            here = place == step * heads + pair * 2 + side
            m_ref[...] = jnp.where(here, peak, m_ref[...])
            l_ref[...] = jnp.where(here, total, l_ref[...])
        o_ref[:, cut] = jnp.where(low_half, outs[0], outs[1])


def far_kernel(sizes, s_ref, q_ref, o_ref, m_ref, l_ref, *rest):
    chips, owned, rank = sizes
    fars, (mine_ref, theirs_ref, all_ref) = rest[:chips], rest[chips:]
    rows = mine_ref.shape[0]
    step = pl.program_id(0)

    @pl.when(step == 0)
    def _():
        for k in range(chips):
            source = lax.bitwise_xor(s_ref[1], k)
            all_ref[pl.ds(pl.multiple_of(source * owned, owned), owned), :] = fars[k][...]

    heads = q_ref.shape[1] // HS
    place = lanes(m_ref.shape)
    for pair in range(heads // 2):
        cut = slice(pair * 128, (pair + 1) * 128)
        qp = q_ref[:, cut]
        low_half = lanes(qp.shape) < HS
        outs, keeps = [], []
        for side in range(2):
            none = jnp.zeros_like(qp)
            qm = jnp.where(low_half, qp, none) if side == 0 else jnp.where(low_half, none, qp)
            head = step * heads + pair * 2 + side
            kv = all_ref[pl.ds(pl.multiple_of(head * rank, rank), rank), :]
            scores = lax.dot_general(qm, kv, NT, preferred_element_type=F32)
            here = place == head
            peak = jnp.sum(jnp.where(here, m_ref[...], 0.0), axis=1, keepdims=True)
            total = jnp.sum(jnp.where(here, l_ref[...], 0.0), axis=1, keepdims=True)
            new = jnp.maximum(peak, jnp.max(scores, axis=1, keepdims=True))
            scores = jnp.exp(scores - new)
            old = jnp.exp(peak - new)
            inverse = 1.0 / (old * total + jnp.sum(scores, axis=1, keepdims=True))
            outs.append(dot(scores.astype(BF), kv) * inverse)
            keeps.append(old * inverse)
        turned = pltpu.roll(jnp.where(low_half, outs[1], outs[0]), 64, 1)
        keep = jnp.where(low_half, keeps[0], keeps[1])
        result = (o_ref[:, cut] * keep + turned).astype(BF)
        mine_ref[:, cut] = result[:rows]
        theirs_ref[:, cut] = result[rows:]


def mix_kernel(s_ref, tok_ref, a_ref, b_ref, wa_ref, wb_ref, mixed_ref, yn_ref):
    total = dot(a_ref[...], wa_ref[...]) + dot(b_ref[...], wb_ref[...])
    mixed = (tok_ref[...].astype(F32) + total).astype(BF)
    mixed_ref[...] = mixed
    yn_ref[...] = layer_norm(mixed.astype(F32)).astype(BF)


def gelu(v):
    return 0.5 * v * (1.0 + jnp.tanh((2.0 / jnp.pi) ** 0.5 * (v + 0.044715 * (v * v * v))))


def feed_kernel(parts, s_ref, yn_ref, *rest):
    sides = len(rest[:-1]) // parts
    out_ref = rest[-1]
    depth = rest[0].shape[1]
    starts = [
        pl.multiple_of(lax.rem(s_ref[4] + parts - i, parts) * depth, depth) for i in range(parts)
    ]
    hidden = []
    for side in range(sides):
        bufs = rest[side * parts : (side + 1) * parts]
        total = sum(dot(yn_ref[:, pl.ds(starts[i], depth)], bufs[i][0]) for i in range(parts))
        hidden.append(gelu(total).astype(BF))
    for i in range(parts):
        total = sum(
            lax.dot_general(hidden[side], rest[side * parts + i][1], NT, preferred_element_type=F32)
            for side in range(sides)
        )
        out_ref[:, pl.ds(starts[i], depth)] = total.astype(out_ref.dtype)


def call(kernel, grid, in_specs, out_specs, out_shape, scratch=(), cost=(0, 0, 0)):
    return pl.pallas_call(
        kernel,
        grid_spec=pltpu.PrefetchScalarGridSpec(
            num_scalar_prefetch=1, grid=grid, in_specs=in_specs, out_specs=out_specs, scratch_shapes=scratch
        ),
        out_shape=out_shape,
        compiler_params=pltpu.CompilerParams(vmem_limit_bytes=VMEM_LIMIT),
        cost_estimate=pl.CostEstimate(flops=cost[0], bytes_accessed=cost[1], transcendentals=cost[2]),
    )


def shape(dims, dtype=BF):
    return jax.ShapeDtypeStruct(dims, dtype)


def whole(dims):
    return pl.BlockSpec(dims, lambda *_: (0,) * len(dims))


def on_device(layer_input, w_qkv, w_out, w_proj, w_up, w_down):
    tokens = layer_input[0]
    rows, width = tokens.shape
    heads, _, rank = w_proj.shape
    n, parts = lax.axis_size("seq"), lax.axis_size("dp")
    chips = n // 2
    me = lax.axis_index("seq")
    core = me % 2
    other = me + 1 - 2 * core
    inner = lambda i: ((i > 0) & (i < n - 1)).astype(jnp.int32)
    scalars = jnp.stack([core, me // 2, inner(me), inner(other), lax.axis_index("dp"), 1 - core]).astype(jnp.int32)

    swap = lambda x: lax.ppermute(x, "seq", [(i, i ^ 1) for i in range(n)])
    jump = lambda x, k: lax.ppermute(x, "seq", [(i, i ^ (2 * k)) for i in range(n)])
    edges = [(i, i + 1) for i in range(1, n - 1, 2)]

    partner = swap(tokens)
    halo = lax.ppermute(tokens, "seq", edges + [(j, i) for i, j in edges])
    halo_partner = swap(halo)

    own = jnp.stack([w_up, w_down])
    weights = [own] + [
        lax.ppermute(own, "dp", [(i, (i + s) % parts) for i in range(parts)]) for s in range(1, parts)
    ]
    partner_weights = [swap(w) for w in weights]

    half = heads // 2
    wide = half * HS
    block = 4 * HS
    steps = wide // block
    owned = half * rank // chips
    extra = max(16, 4 * owned // 128)
    blocks = width // block
    tok_spec = whole((rows, width))
    column = lambda which: pl.BlockSpec(
        (width, block), lambda g, s, which=which: (0, which * blocks + s[0] * steps + g)
    )
    proj_spec = pl.BlockSpec((4, HS, rank), lambda g, s: (s[0] * steps + g, 0, 0))
    slab = pl.BlockSpec((2 * rows, block), lambda g, s: (0, g))
    out = call(
        functools.partial(qkv_kernel, (chips, owned, extra, steps, rank)),
        (steps,),
        [tok_spec, tok_spec, column(0), column(1), column(2), proj_spec],
        [slab, slab, slab] + [pl.BlockSpec(memory_space=pl.ANY)] * chips,
        [shape((2 * rows, wide))] * 3 + [shape((owned + extra, 128))] * chips,
        [
            pltpu.VMEM((2 * rows, width), BF),
            pltpu.VMEM((chips, owned + extra, 128), BF),
            pltpu.SemaphoreType.DMA((chips,)),
        ],
        (4 * rows * width * 3 * wide, 6 * width * wide, half * rank * 2 * rows),
    )(scalars, tokens, partner, w_qkv, w_qkv, w_qkv, w_proj)
    query, near_keys, near_values = out[:3]
    pays = [out[3]] + [jump(out[3 + k], k) for k in range(1, chips)]

    near, peaks, totals = call(
        near_kernel,
        (steps,),
        [slab, slab, slab, tok_spec, tok_spec, column(1), column(2)],
        [slab, whole((2 * rows, 128)), whole((2 * rows, 128))],
        [shape((2 * rows, wide), F32), shape((2 * rows, 128), F32), shape((2 * rows, 128), F32)],
        [pltpu.VMEM((2 * rows, width), BF)],
        (4 * rows * width * 2 * wide, 6 * width * wide, half * 3 * WBLK * 2 * rows),
    )(scalars, query, near_keys, near_values, halo, halo_partner, w_qkv, w_qkv)

    far = pl.pallas_call(
        functools.partial(combine_kernel, (chips, owned, extra)),
        out_shape=shape((owned, 128)),
        cost_estimate=pl.CostEstimate(flops=1000000, bytes_accessed=1000000, transcendentals=0),
    )(*pays)
    fars = [far] + [jump(far, k) for k in range(1, chips)]
    piece = pl.BlockSpec((rows, block), lambda g, s: (0, g))
    mine, theirs = call(
        functools.partial(far_kernel, (chips, owned, rank)),
        (steps,),
        [slab, slab, whole((2 * rows, 128)), whole((2 * rows, 128))] + [whole((owned, 128))] * chips,
        [piece, piece],
        [shape((rows, wide))] * 2,
        [pltpu.VMEM((half * rank, 128), BF)],
        (4 * rows * wide * rank * 2, 6 * rows * wide, half * rank * 2 * rows),
    )(scalars, query, near, peaks, totals, *fars)
    arrived = swap(theirs)
    mixed, yn = call(
        mix_kernel,
        (1,),
        [
            tok_spec,
            whole((rows, wide)),
            whole((rows, wide)),
            pl.BlockSpec((wide, width), lambda g, s: (s[0], 0)),
            pl.BlockSpec((wide, width), lambda g, s: (s[5], 0)),
        ],
        [tok_spec, tok_spec],
        [shape((rows, width))] * 2,
        (),
        (4 * rows * width * wide, 2 * width * width, 0),
    )(scalars, tokens, mine, arrived, w_out, w_out)

    bufs = weights + partner_weights
    feed = lambda x, dtype: call(
        functools.partial(feed_kernel, parts),
        (1,),
        [tok_spec] + [whole(own.shape)] * len(bufs),
        tok_spec,
        shape((rows, width), dtype),
        (),
        (8 * rows * width * 2 * w_up.shape[1], 8 * width * w_up.shape[1], rows * 2 * w_up.shape[1]),
    )(scalars, x, *bufs)
    visitors = [jump(yn, k) for k in range(1, chips)]
    result = mixed.astype(F32) + feed(yn, F32)
    for k, x in enumerate(visitors, 1):
        result = result + jump(feed(x, BF), k).astype(F32)
    return result.astype(BF)[None]


def solution(mesh):
    in_specs = (P("dp", "seq", None), P(), P(), P(), P("dp", "seq"), P("dp", "seq"))
    out_specs = P("dp", "seq", None)
    return jax.shard_map(
        on_device, mesh=mesh, in_specs=in_specs, out_specs=out_specs, check_vma=False
    )
```

```python
import functools

import jax
import jax.numpy as jnp
from jax import lax
from jax.experimental import pallas as pl
from jax.experimental.pallas import tpu as pltpu
from jax.sharding import PartitionSpec as P


HS = 64
WBLK = 256
EPS = 1e-05
F32 = jnp.float32
BF = jnp.bfloat16
NT = (((1,), (1,)), ((), ()))
TT = (((0,), (1,)), ((), ()))
VMEM_LIMIT = 24 * 1024 * 1024
SMALL = 60.0


def dot(a, b):
    return jnp.dot(a, b, preferred_element_type=F32)


def layer_norm(x):
    center = x - jnp.mean(x, axis=-1, keepdims=True)
    spread = jnp.mean(center * center, axis=-1, keepdims=True)
    return center * lax.rsqrt(spread + EPS)


def head_average(width):
    a = lax.broadcasted_iota(jnp.int32, (width, width), 0) // HS
    b = lax.broadcasted_iota(jnp.int32, (width, width), 1) // HS
    return jnp.where(a == b, 1.0 / HS, 0.0).astype(F32)


def split(x):
    high = x.astype(BF)
    return high, (x - high.astype(F32)).astype(BF)


def head_norm(x):
    avg = head_average(x.shape[1]).astype(BF)
    center = x.astype(F32) - dot(x, avg)
    spread = dot((center * center).astype(BF), avg)
    return (center * lax.rsqrt(spread + EPS)).astype(BF)


def head_sum(x):
    square = x.astype(F32) * x.astype(F32)
    return dot(square.astype(BF), head_average(x.shape[1]).astype(BF)) * HS


def head_norm_wide(x):
    avg = head_average(x.shape[1]).astype(BF)

    def mean(y):
        one = y.astype(BF)
        rest = y - one.astype(F32)
        two, three = split(rest)
        return dot(one, avg) + dot(two, avg) + dot(three, avg)

    center = x - mean(x)
    spread = mean(center * center)
    return (center * lax.rsqrt(spread + EPS)).astype(BF)


def lanes(shape):
    return lax.broadcasted_iota(jnp.int32, shape, len(shape) - 1)


def diagonal(size):
    return lax.broadcasted_iota(jnp.int32, (size, size), 0) == lax.broadcasted_iota(
        jnp.int32, (size, size), 1
    )


def to_row(column):
    size = column.shape[0]
    return jnp.sum(jnp.where(diagonal(size), column, 0.0), axis=0, keepdims=True)


def to_column(row):
    size = row.shape[1]
    return jnp.sum(jnp.where(diagonal(size), row, 0.0), axis=1, keepdims=True)


def qkv_kernel(sizes, s_ref, tok_ref, par_ref, wq_ref, wk_ref, wv_ref, wp_ref, q_ref, nk_ref, nv_ref, top_ref, *rest):
    chips, owned, extra, steps, rank = sizes
    pays, (xn_ref, pay_ref, sem) = rest[:chips], rest[chips:]
    rows = tok_ref.shape[0]
    step = pl.program_id(0)

    @pl.when(step == 0)
    def _():
        xn_ref[:rows] = layer_norm(tok_ref[...].astype(F32)).astype(BF)
        xn_ref[rows:] = layer_norm(par_ref[...].astype(F32)).astype(BF)
        top_ref[...] = jnp.zeros_like(top_ref)

    x = xn_ref[...]
    kk = dot(x, wk_ref[...]).astype(BF)
    vv = dot(x, wv_ref[...]).astype(BF)
    width = kk.shape[1]
    heads = width // HS
    owners = heads * rank // owned
    stat_rows = owned // 128
    place = lax.broadcasted_iota(jnp.int32, (extra, 128), 0)

    def partial_sums(shifted):
        stats = [jnp.zeros((extra, 128), F32) for _ in range(owners)]
        for pair in range(heads // 2):
            kp = kk[:, pair * 128 : (pair + 1) * 128]
            vp = vv[:, pair * 128 : (pair + 1) * 128]
            turned = pltpu.roll(vp.astype(F32), 64, 1).astype(BF)
            low_half = lanes(kp.shape) < HS
            for side in range(2):
                head = pair * 2 + side
                mixed = jnp.where(low_half, kp, turned) if side == 0 else jnp.where(low_half, turned, kp)
                wp = wp_ref[head]
                none = jnp.zeros_like(wp)
                wide = jnp.concatenate([wp, none] if side == 0 else [none, wp], axis=0)
                logits = lax.dot_general(wide, kp, TT, preferred_element_type=F32)
                if shifted:
                    peak = jnp.max(logits, axis=1, keepdims=True)
                    logits = logits - peak
                weight = jnp.exp(logits).astype(BF)
                total = jnp.sum(weight.astype(F32), axis=1, keepdims=True)
                sums = dot(weight, mixed).astype(BF)
                for part in range(rank // 128):
                    column = head * rank + part * 128
                    owner, offset = column // owned, column % owned
                    cut = slice(part * 128, (part + 1) * 128)
                    pay_ref[step * owners + owner, offset : offset + 128, :] = sums[cut]
                    entries = [(3, to_row(total[cut]))]
                    if shifted:
                        one = to_row(peak[cut])
                        first = one.astype(BF).astype(F32)
                        second = (one - first).astype(BF).astype(F32)
                        entries += [(0, first), (1, second), (2, one - first - second)]
                    for i, row in entries:
                        stats[owner] = jnp.where(place == i * stat_rows + offset // 128, row, stats[owner])
        for owner in range(owners):
            pay_ref[step * owners + owner, owned : owned + extra, :] = stats[owner].astype(BF)

    key_norm = jnp.max(head_sum(kk))
    column_norm = jnp.max(jnp.sum(jnp.square(wp_ref[...].astype(F32)), axis=1))
    near_zero = key_norm * column_norm < SMALL * SMALL
    pl.when(near_zero)(lambda: partial_sums(False))
    pl.when(jnp.logical_not(near_zero))(lambda: partial_sums(True))
    nk_ref[...] = head_norm(kk)
    nv_ref[...] = head_norm(vv)
    query = (dot(x, wq_ref[...]).astype(BF).astype(F32) * HS ** (-0.5)).astype(BF)
    q_ref[...] = query
    top_ref[...] = jnp.maximum(top_ref[...], jnp.max(head_sum(query)))

    @pl.when(step == steps - 1)
    def _():
        chip = s_ref[1]
        copies = [
            pltpu.make_async_copy(pay_ref.at[lax.bitwise_xor(chip, k)], pays[k], sem.at[k]) for k in range(chips)
        ]
        for copy in copies:
            copy.start()
        for copy in copies:
            copy.wait()


def combine_kernel(sizes, *refs):
    chips, owned, extra = sizes
    pays, far_ref = refs[:chips], refs[chips]
    stat_rows = owned // 128
    tails = [p[owned : owned + extra, :].astype(F32) for p in pays]
    peaks = [
        t[:stat_rows] + t[stat_rows : 2 * stat_rows] + t[2 * stat_rows : 3 * stat_rows] for t in tails
    ]
    peak = functools.reduce(jnp.maximum, peaks)
    scales = [jnp.exp(p - peak) for p in peaks]
    total = sum(s * t[3 * stat_rows : 4 * stat_rows] for s, t in zip(scales, tails))
    scales = [s / total for s in scales]
    for i in range(stat_rows):
        cut = slice(i * 128, (i + 1) * 128)
        summary = sum(to_column(s[i : i + 1]) * p[cut, :].astype(F32) for s, p in zip(scales, pays))
        far_ref[cut, :] = head_norm_wide(summary)


def one_head(qp, side):
    low_half = lanes(qp.shape) < HS
    none = jnp.zeros_like(qp)
    return jnp.where(low_half, qp, none) if side == 0 else jnp.where(low_half, none, qp)


def with_ones(v, side):
    low_half = lanes(v.shape) < HS
    ones = jnp.ones_like(v)
    return jnp.where(low_half, v, ones) if side == 0 else jnp.where(low_half, ones, v)


def small_scores(top_ref):
    return jnp.max(top_ref[...]) * (HS * 1.02) < SMALL * SMALL


def near_kernel(s_ref, top_ref, q_ref, nk_ref, nv_ref, halo_ref, halop_ref, wk_ref, wv_ref, o_ref, m_ref, xh_ref):
    rows = halo_ref.shape[0]
    step = pl.program_id(0)

    @pl.when(step == 0)
    def _():
        xh_ref[:rows] = layer_norm(halo_ref[...].astype(F32)).astype(BF)
        xh_ref[rows:] = layer_norm(halop_ref[...].astype(F32)).astype(BF)
        m_ref[...] = jnp.zeros_like(m_ref)

    x = xh_ref[...]
    halo_k = head_norm(dot(x, wk_ref[...]).astype(BF))
    halo_v = head_norm(dot(x, wv_ref[...]).astype(BF))
    inside = [s_ref[i] > 0 for i in (2, 3)]
    heads = halo_k.shape[1] // HS
    place = lanes((rows, 128))

    def attend(shifted):
        for pair in range(heads // 2):
            cut = slice(pair * 128, (pair + 1) * 128)
            kp = nk_ref[:, cut]
            for side in range(2):
                vp = with_ones(nv_ref[:, cut], side)
                for part in range(2):
                    these = slice(part * rows, (part + 1) * rows)
                    qm = one_head(q_ref[these, cut], side)
                    main = lax.dot_general(qm, kp, NT, preferred_element_type=F32)
                    halo = lax.dot_general(qm, halo_k[these, cut], NT, preferred_element_type=F32)
                    halo = halo + jnp.where(inside[part], 0.0, -jnp.inf).astype(F32)
                    if shifted:
                        peak = jnp.maximum(
                            jnp.max(main, axis=1, keepdims=True), jnp.max(halo, axis=1, keepdims=True)
                        )
                        main, halo = main - peak, halo - peak
                        here = place == step * heads + pair * 2 + side
                        m_ref[these] = jnp.where(here, peak, m_ref[these])
                    out = dot(jnp.exp(main).astype(BF), vp)
                    out = out + dot(jnp.exp(halo).astype(BF), with_ones(halo_v[these, cut], side))
                    o_ref[these, (pair * 2 + side) * 128 : (pair * 2 + side + 1) * 128] = out

    small = small_scores(top_ref)
    pl.when(small)(lambda: attend(False))
    pl.when(jnp.logical_not(small))(lambda: attend(True))


def far_kernel(sizes, s_ref, top_ref, q_ref, o_ref, m_ref, *rest):
    chips, owned, rank = sizes
    fars, (mine_ref, theirs_ref, all_ref) = rest[:chips], rest[chips:]
    rows = mine_ref.shape[0]
    step = pl.program_id(0)

    @pl.when(step == 0)
    def _():
        for k in range(chips):
            source = lax.bitwise_xor(s_ref[1], k)
            all_ref[pl.ds(pl.multiple_of(source * owned, owned), owned), :] = fars[k][...]

    heads = q_ref.shape[1] // HS
    place = lanes((rows, 128))

    def attend(shifted):
        for pair in range(heads // 2):
            cut = slice(pair * 128, (pair + 1) * 128)
            for part in range(2):
                these = slice(part * rows, (part + 1) * rows)
                low_half = lanes((rows, 128)) < HS
                sums = []
                for side in range(2):
                    qm = one_head(q_ref[these, cut], side)
                    head = step * heads + pair * 2 + side
                    kv = all_ref[pl.ds(pl.multiple_of(head * rank, rank), rank), :]
                    scores = lax.dot_general(qm, kv, NT, preferred_element_type=F32)
                    before = o_ref[these, (pair * 2 + side) * 128 : (pair * 2 + side + 1) * 128]
                    if shifted:
                        peak = jnp.sum(jnp.where(place == head, m_ref[these], 0.0), axis=1, keepdims=True)
                        new = jnp.maximum(peak, jnp.max(scores, axis=1, keepdims=True))
                        scores = scores - new
                        before = before * jnp.exp(peak - new)
                    out = dot(jnp.exp(scores).astype(BF), with_ones(kv, 1 - side))
                    sums.append(before + pltpu.roll(out, 64, 1))
                total = pltpu.roll(jnp.where(low_half, sums[1], sums[0]), 64, 1)
                result = (jnp.where(low_half, sums[0], sums[1]) / total).astype(BF)
                (mine_ref, theirs_ref)[part][:, cut] = result

    small = small_scores(top_ref)
    pl.when(small)(lambda: attend(False))
    pl.when(jnp.logical_not(small))(lambda: attend(True))


def mix_kernel(s_ref, tok_ref, a_ref, b_ref, w_ref, mixed_ref, yn_ref):
    wide = a_ref.shape[1]
    first = pl.ds(pl.multiple_of(s_ref[0] * wide, wide), wide)
    second = pl.ds(pl.multiple_of(s_ref[5] * wide, wide), wide)
    total = dot(a_ref[...], w_ref[first, :]) + dot(b_ref[...], w_ref[second, :])
    mixed = (tok_ref[...].astype(F32) + total).astype(BF)
    mixed_ref[...] = mixed
    yn_ref[...] = layer_norm(mixed.astype(F32)).astype(BF)


def gelu(v):
    return 0.5 * v * (1.0 + jnp.tanh((2.0 / jnp.pi) ** 0.5 * (v + 0.044715 * (v * v * v))))


def feed_kernel(parts, s_ref, yn_ref, *rest):
    sides = len(rest[:-1]) // parts
    out_ref = rest[-1]
    depth = rest[0].shape[1]
    starts = [
        pl.multiple_of(lax.rem(s_ref[4] + parts - i, parts) * depth, depth) for i in range(parts)
    ]
    hidden = []
    for side in range(sides):
        bufs = rest[side * parts : (side + 1) * parts]
        total = sum(dot(yn_ref[:, pl.ds(starts[i], depth)], bufs[i][0]) for i in range(parts))
        hidden.append(gelu(total).astype(BF))
    for i in range(parts):
        total = sum(
            lax.dot_general(hidden[side], rest[side * parts + i][1], NT, preferred_element_type=F32)
            for side in range(sides)
        )
        out_ref[:, pl.ds(starts[i], depth)] = total.astype(out_ref.dtype)


def call(kernel, grid, in_specs, out_specs, out_shape, scratch=(), cost=(0, 0, 0)):
    return pl.pallas_call(
        kernel,
        grid_spec=pltpu.PrefetchScalarGridSpec(
            num_scalar_prefetch=1, grid=grid, in_specs=in_specs, out_specs=out_specs, scratch_shapes=scratch
        ),
        out_shape=out_shape,
        compiler_params=pltpu.CompilerParams(vmem_limit_bytes=VMEM_LIMIT),
        cost_estimate=pl.CostEstimate(flops=cost[0], bytes_accessed=cost[1], transcendentals=cost[2]),
    )


def shape(dims, dtype=BF):
    return jax.ShapeDtypeStruct(dims, dtype)


def whole(dims):
    return pl.BlockSpec(dims, lambda *_: (0,) * len(dims))


def after(x, *earlier):
    return lax.optimization_barrier((x,) + earlier)[0]


def on_device(layer_input, w_qkv, w_out, w_proj, w_up, w_down):
    tokens = layer_input[0]
    rows, width = tokens.shape
    heads, _, rank = w_proj.shape
    n, parts = lax.axis_size("seq"), lax.axis_size("dp")
    chips = n // 2
    me = lax.axis_index("seq")
    core = me % 2
    other = me + 1 - 2 * core
    inner = lambda i: ((i > 0) & (i < n - 1)).astype(jnp.int32)
    scalars = jnp.stack([core, me // 2, inner(me), inner(other), lax.axis_index("dp"), 1 - core]).astype(jnp.int32)
    vmem = pl.BlockSpec(memory_space=pltpu.VMEM)

    swap = lambda x: lax.ppermute(x, "seq", [(i, i ^ 1) for i in range(n)])
    jump = lambda x, k: lax.ppermute(x, "seq", [(i, i ^ (2 * k)) for i in range(n)])
    edges = [(i, i + 1) for i in range(1, n - 1, 2)]

    partner = swap(tokens)
    halo = lax.ppermute(tokens, "seq", edges + [(j, i) for i, j in edges])

    own = jnp.stack([w_up, w_down])
    gathered = [own]
    for s in range(1, parts):
        gathered.append(lax.ppermute(own, "dp", [(i, (i + s) % parts) for i in range(parts)]))
    share = chips // 2
    shared = []

    def share_part(s, *earlier):
        if share and s < parts:
            shared.append(jump(after(gathered[s], *earlier) if earlier else gathered[s], share))

    share_part(0)
    w_qkv = pltpu.with_memory_space_constraint(w_qkv, pltpu.HBM)

    half = heads // 2
    wide = half * HS
    block = 4 * HS
    steps = wide // block
    owned = half * rank // chips
    extra = max(16, 4 * owned // 128)
    blocks = width // block
    tok_spec = whole((rows, width))
    column = lambda which: pl.BlockSpec(
        (width, block), lambda g, s, which=which: (0, which * blocks + s[0] * steps + g)
    )
    proj_spec = pl.BlockSpec((4, HS, rank), lambda g, s: (s[0] * steps + g, 0, 0))
    slab = pl.BlockSpec((2 * rows, block), lambda g, s: (0, g))
    out = call(
        functools.partial(qkv_kernel, (chips, owned, extra, steps, rank)),
        (steps,),
        [tok_spec, tok_spec, column(0), column(1), column(2), proj_spec],
        [slab, slab, slab, whole((8, 128))] + [pl.BlockSpec(memory_space=pl.ANY)] * chips,
        [shape((2 * rows, wide))] * 3 + [shape((8, 128), F32)] + [shape((owned + extra, 128))] * chips,
        [
            pltpu.VMEM((2 * rows, width), BF),
            pltpu.VMEM((chips, owned + extra, 128), BF),
            pltpu.SemaphoreType.DMA((chips,)),
        ],
        (4 * rows * width * 3 * wide, 6 * width * wide, half * rank * 2 * rows),
    )(scalars, tokens, partner, w_qkv, w_qkv, w_qkv, w_proj)
    query, near_keys, near_values, top = out[:4]
    pays = [out[4]] + [jump(out[4 + k], k) for k in range(1, chips)]

    halo = after(halo, out[4])
    halo_partner = swap(halo)
    share_part(1, out[4])
    per_head = pl.BlockSpec((2 * rows, 2 * block), lambda g, s: (0, g))
    near, peaks = call(
        near_kernel,
        (steps,),
        [whole((8, 128)), slab, slab, slab, tok_spec, tok_spec, column(1), column(2)],
        [per_head, whole((2 * rows, 128))],
        [shape((2 * rows, 2 * wide), F32), shape((2 * rows, 128), F32)],
        [pltpu.VMEM((2 * rows, width), BF)],
        (4 * rows * width * 2 * wide, 6 * width * wide, half * 3 * WBLK * 2 * rows),
    )(scalars, top, query, near_keys, near_values, halo, halo_partner, w_qkv, w_qkv)

    pays = [after(p, near) for p in pays]
    far = pl.pallas_call(
        functools.partial(combine_kernel, (chips, owned, extra)),
        out_shape=shape((owned, 128)),
        compiler_params=pltpu.CompilerParams(vmem_limit_bytes=VMEM_LIMIT),
        cost_estimate=pl.CostEstimate(flops=1000000, bytes_accessed=1000000, transcendentals=0),
    )(*pays)
    own_sides = gathered + [swap(after(w, far)) for w in gathered]
    share_part(2, far)
    fars = [far] + [jump(far, k) for k in range(1, chips)]
    mine, theirs = call(
        functools.partial(far_kernel, (chips, owned, rank)),
        (steps,),
        [whole((8, 128)), slab, per_head, whole((2 * rows, 128))] + [whole((owned, 128))] * chips,
        [pl.BlockSpec((rows, block), lambda g, s: (0, g))] * 2,
        [shape((rows, wide))] * 2,
        [pltpu.VMEM((half * rank, 128), BF)],
        (4 * rows * wide * rank * 2, 6 * rows * wide, half * rank * 2 * rows),
    )(scalars, top, query, near, peaks, *fars)
    arrived = swap(theirs)
    for s in range(3, parts):
        share_part(s, theirs)
    mixed, yn = call(
        mix_kernel,
        (1,),
        [vmem] * 4,
        [vmem] * 2,
        [shape((rows, width))] * 2,
        (),
        (4 * rows * width * wide, 2 * width * width, 0),
    )(scalars, tokens, mine, arrived, w_out)


    def feed(x, dtype, weights):
        return call(
            functools.partial(feed_kernel, parts),
            (1,),
            [vmem] * (1 + len(weights)),
            vmem,
            shape((rows, width), dtype),
            (),
            (2 * rows * width * len(weights) * w_up.shape[1], len(weights) * own.size, rows * w_up.shape[1]),
        )(scalars, x, *weights)

    visits = range(1, max(share, 1))
    visitors = []
    for k in visits:
        visitors.append(jump(yn, k))
    terms = [feed(yn, F32, own_sides)]
    all_sides = own_sides
    if share:
        shared = [after(w, terms[0]) for w in shared]
        far_sides = shared + [swap(w) for w in shared]
        all_sides = own_sides + far_sides
    returned = []
    for k, x in zip(visits, visitors):
        x = feed(after(x, terms[0]), BF, all_sides)
        returned.append(jump(x, k))
    if share:
        terms.append(feed(after(yn, x) if returned else yn, F32, far_sides))
    result = mixed.astype(F32) + sum(terms)
    for x in returned:
        result = result + x.astype(F32)
    return result.astype(BF)[None]


def solution(mesh):
    in_specs = (P("dp", "seq", None), P(), P(), P(), P("dp", "seq"), P("dp", "seq"))
    out_specs = P("dp", "seq", None)
    return jax.shard_map(on_device, mesh=mesh, in_specs=in_specs, out_specs=out_specs, check_vma=False)
```

```python
import functools

import jax
import jax.numpy as jnp
from jax import lax
from jax.experimental import pallas as pl
from jax.experimental.pallas import tpu as pltpu
from jax.sharding import PartitionSpec as P


HS = 64
WBLK = 256
EPS = 1e-05
F32 = jnp.float32
BF = jnp.bfloat16
NT = (((1,), (1,)), ((), ()))
TT = (((0,), (1,)), ((), ()))
VMEM_LIMIT = 24 * 1024 * 1024
SMALL = 60.0


def dot(a, b):
    return jnp.dot(a, b, preferred_element_type=F32)


def layer_norm(x):
    center = x - jnp.mean(x, axis=-1, keepdims=True)
    spread = jnp.mean(center * center, axis=-1, keepdims=True)
    return center * lax.rsqrt(spread + EPS)


def head_average(width):
    a = lax.broadcasted_iota(jnp.int32, (width, width), 0) // HS
    b = lax.broadcasted_iota(jnp.int32, (width, width), 1) // HS
    return jnp.where(a == b, 1.0 / HS, 0.0).astype(F32)


def split(x):
    high = x.astype(BF)
    return high, (x - high.astype(F32)).astype(BF)


def head_norm(x):
    avg = head_average(x.shape[1]).astype(BF)
    center = x.astype(F32) - dot(x, avg)
    spread = dot((center * center).astype(BF), avg)
    return (center * lax.rsqrt(spread + EPS)).astype(BF)


def head_sum(x):
    square = x.astype(F32) * x.astype(F32)
    return dot(square.astype(BF), head_average(x.shape[1]).astype(BF)) * HS


def head_norm_wide(x):
    avg = head_average(x.shape[1]).astype(BF)

    def mean(y):
        one = y.astype(BF)
        rest = y - one.astype(F32)
        two, three = split(rest)
        return dot(one, avg) + dot(two, avg) + dot(three, avg)

    center = x - mean(x)
    spread = mean(center * center)
    return (center * lax.rsqrt(spread + EPS)).astype(BF)


def lanes(shape):
    return lax.broadcasted_iota(jnp.int32, shape, len(shape) - 1)


def diagonal(size):
    return lax.broadcasted_iota(jnp.int32, (size, size), 0) == lax.broadcasted_iota(
        jnp.int32, (size, size), 1
    )


def to_row(column):
    size = column.shape[0]
    return jnp.sum(jnp.where(diagonal(size), column, 0.0), axis=0, keepdims=True)


def to_column(row):
    size = row.shape[1]
    return jnp.sum(jnp.where(diagonal(size), row, 0.0), axis=1, keepdims=True)


def qkv_kernel(sizes, s_ref, tok_ref, par_ref, wq_ref, wk_ref, wv_ref, wp_ref, q_ref, nk_ref, nv_ref, top_ref, *rest):
    chips, owned, extra, steps, rank = sizes
    pays, (xn_ref, pay_ref, sem) = rest[:chips], rest[chips:]
    rows = tok_ref.shape[0]
    step = pl.program_id(0)

    @pl.when(step == 0)
    def _():
        xn_ref[:rows] = layer_norm(tok_ref[...].astype(F32)).astype(BF)
        xn_ref[rows:] = layer_norm(par_ref[...].astype(F32)).astype(BF)
        top_ref[...] = jnp.zeros_like(top_ref)

    x = xn_ref[...]
    kk = dot(x, wk_ref[...]).astype(BF)
    vv = dot(x, wv_ref[...]).astype(BF)
    width = kk.shape[1]
    heads = width // HS
    owners = heads * rank // owned
    stat_rows = owned // 128
    place = lax.broadcasted_iota(jnp.int32, (extra, 128), 0)

    def partial_sums(shifted):
        stats = [jnp.zeros((extra, 128), F32) for _ in range(owners)]
        for pair in range(heads // 2):
            kp = kk[:, pair * 128 : (pair + 1) * 128]
            vp = vv[:, pair * 128 : (pair + 1) * 128]
            turned = pltpu.roll(vp.astype(F32), 64, 1).astype(BF)
            low_half = lanes(kp.shape) < HS
            for side in range(2):
                head = pair * 2 + side
                mixed = jnp.where(low_half, kp, turned) if side == 0 else jnp.where(low_half, turned, kp)
                wp = wp_ref[head]
                none = jnp.zeros_like(wp)
                wide = jnp.concatenate([wp, none] if side == 0 else [none, wp], axis=0)
                logits = lax.dot_general(wide, kp, TT, preferred_element_type=F32)
                if shifted:
                    peak = jnp.max(logits, axis=1, keepdims=True)
                    logits = logits - peak
                weight = jnp.exp(logits).astype(BF)
                total = jnp.sum(weight.astype(F32), axis=1, keepdims=True)
                sums = dot(weight, mixed).astype(BF)
                for part in range(rank // 128):
                    column = head * rank + part * 128
                    owner, offset = column // owned, column % owned
                    cut = slice(part * 128, (part + 1) * 128)
                    pay_ref[step * owners + owner, offset : offset + 128, :] = sums[cut]
                    entries = [(3, to_row(total[cut]))]
                    if shifted:
                        one = to_row(peak[cut])
                        first = one.astype(BF).astype(F32)
                        second = (one - first).astype(BF).astype(F32)
                        entries += [(0, first), (1, second), (2, one - first - second)]
                    for i, row in entries:
                        stats[owner] = jnp.where(place == i * stat_rows + offset // 128, row, stats[owner])
        for owner in range(owners):
            pay_ref[step * owners + owner, owned : owned + extra, :] = stats[owner].astype(BF)

    key_norm = jnp.max(head_sum(kk))
    column_norm = jnp.max(jnp.sum(jnp.square(wp_ref[...].astype(F32)), axis=1))
    near_zero = key_norm * column_norm < SMALL * SMALL
    pl.when(near_zero)(lambda: partial_sums(False))
    pl.when(jnp.logical_not(near_zero))(lambda: partial_sums(True))
    nk_ref[...] = head_norm(kk)
    nv_ref[...] = head_norm(vv)
    query = (dot(x, wq_ref[...]).astype(BF).astype(F32) * HS ** (-0.5)).astype(BF)
    q_ref[...] = query
    top_ref[...] = jnp.maximum(top_ref[...], jnp.max(head_sum(query)))

    @pl.when(step == steps - 1)
    def _():
        chip = s_ref[1]
        copies = [
            pltpu.make_async_copy(pay_ref.at[lax.bitwise_xor(chip, k)], pays[k], sem.at[k]) for k in range(chips)
        ]
        for copy in copies:
            copy.start()
        for copy in copies:
            copy.wait()


def combine_kernel(sizes, *refs):
    chips, owned, extra = sizes
    pays, far_ref = refs[:chips], refs[chips]
    stat_rows = owned // 128
    tails = [p[owned : owned + extra, :].astype(F32) for p in pays]
    peaks = [
        t[:stat_rows] + t[stat_rows : 2 * stat_rows] + t[2 * stat_rows : 3 * stat_rows] for t in tails
    ]
    peak = functools.reduce(jnp.maximum, peaks)
    scales = [jnp.exp(p - peak) for p in peaks]
    total = sum(s * t[3 * stat_rows : 4 * stat_rows] for s, t in zip(scales, tails))
    scales = [s / total for s in scales]
    for i in range(stat_rows):
        cut = slice(i * 128, (i + 1) * 128)
        summary = sum(to_column(s[i : i + 1]) * p[cut, :].astype(F32) for s, p in zip(scales, pays))
        far_ref[cut, :] = head_norm_wide(summary)


def one_head(qp, side):
    low_half = lanes(qp.shape) < HS
    none = jnp.zeros_like(qp)
    return jnp.where(low_half, qp, none) if side == 0 else jnp.where(low_half, none, qp)


def with_ones(v, side):
    low_half = lanes(v.shape) < HS
    ones = jnp.ones_like(v)
    return jnp.where(low_half, v, ones) if side == 0 else jnp.where(low_half, ones, v)


def small_scores(top_ref):
    return jnp.max(top_ref[...]) * (HS * 1.02) < SMALL * SMALL


def near_kernel(s_ref, top_ref, q_ref, nk_ref, nv_ref, halo_ref, halop_ref, wk_ref, wv_ref, o_ref, m_ref, xh_ref):
    rows = halo_ref.shape[0]
    step = pl.program_id(0)

    @pl.when(step == 0)
    def _():
        xh_ref[:rows] = layer_norm(halo_ref[...].astype(F32)).astype(BF)
        xh_ref[rows:] = layer_norm(halop_ref[...].astype(F32)).astype(BF)
        m_ref[...] = jnp.zeros_like(m_ref)

    x = xh_ref[...]
    halo_k = head_norm(dot(x, wk_ref[...]).astype(BF))
    halo_v = head_norm(dot(x, wv_ref[...]).astype(BF))
    inside = [s_ref[i] > 0 for i in (2, 3)]
    heads = halo_k.shape[1] // HS
    place = lanes((rows, 128))

    def attend(shifted):
        for pair in range(heads // 2):
            cut = slice(pair * 128, (pair + 1) * 128)
            kp = nk_ref[:, cut]
            for side in range(2):
                vp = with_ones(nv_ref[:, cut], side)
                for part in range(2):
                    these = slice(part * rows, (part + 1) * rows)
                    qm = one_head(q_ref[these, cut], side)
                    main = lax.dot_general(qm, kp, NT, preferred_element_type=F32)
                    halo = lax.dot_general(qm, halo_k[these, cut], NT, preferred_element_type=F32)
                    halo = halo + jnp.where(inside[part], 0.0, -jnp.inf).astype(F32)
                    if shifted:
                        peak = jnp.maximum(
                            jnp.max(main, axis=1, keepdims=True), jnp.max(halo, axis=1, keepdims=True)
                        )
                        main, halo = main - peak, halo - peak
                        here = place == step * heads + pair * 2 + side
                        m_ref[these] = jnp.where(here, peak, m_ref[these])
                    out = dot(jnp.exp(main).astype(BF), vp)
                    out = out + dot(jnp.exp(halo).astype(BF), with_ones(halo_v[these, cut], side))
                    o_ref[these, (pair * 2 + side) * 128 : (pair * 2 + side + 1) * 128] = out

    small = small_scores(top_ref)
    pl.when(small)(lambda: attend(False))
    pl.when(jnp.logical_not(small))(lambda: attend(True))


def far_kernel(sizes, s_ref, top_ref, q_ref, o_ref, m_ref, *rest):
    chips, owned, rank = sizes
    fars, (mine_ref, theirs_ref, all_ref) = rest[:chips], rest[chips:]
    rows = mine_ref.shape[0]
    step = pl.program_id(0)

    @pl.when(step == 0)
    def _():
        for k in range(chips):
            source = lax.bitwise_xor(s_ref[1], k)
            all_ref[pl.ds(pl.multiple_of(source * owned, owned), owned), :] = fars[k][...]

    heads = q_ref.shape[1] // HS
    place = lanes((rows, 128))

    def attend(shifted):
        for pair in range(heads // 2):
            cut = slice(pair * 128, (pair + 1) * 128)
            for part in range(2):
                these = slice(part * rows, (part + 1) * rows)
                low_half = lanes((rows, 128)) < HS
                sums = []
                for side in range(2):
                    qm = one_head(q_ref[these, cut], side)
                    head = step * heads + pair * 2 + side
                    kv = all_ref[pl.ds(pl.multiple_of(head * rank, rank), rank), :]
                    scores = lax.dot_general(qm, kv, NT, preferred_element_type=F32)
                    before = o_ref[these, (pair * 2 + side) * 128 : (pair * 2 + side + 1) * 128]
                    if shifted:
                        peak = jnp.sum(jnp.where(place == head, m_ref[these], 0.0), axis=1, keepdims=True)
                        new = jnp.maximum(peak, jnp.max(scores, axis=1, keepdims=True))
                        scores = scores - new
                        before = before * jnp.exp(peak - new)
                    out = dot(jnp.exp(scores).astype(BF), with_ones(kv, 1 - side))
                    sums.append(before + pltpu.roll(out, 64, 1))
                total = pltpu.roll(jnp.where(low_half, sums[1], sums[0]), 64, 1)
                result = (jnp.where(low_half, sums[0], sums[1]) / total).astype(BF)
                (mine_ref, theirs_ref)[part][:, cut] = result

    small = small_scores(top_ref)
    pl.when(small)(lambda: attend(False))
    pl.when(jnp.logical_not(small))(lambda: attend(True))


def mix_kernel(s_ref, tok_ref, a_ref, b_ref, w_ref, mixed_ref, yn_ref):
    wide = a_ref.shape[1]
    first = pl.ds(pl.multiple_of(s_ref[0] * wide, wide), wide)
    second = pl.ds(pl.multiple_of(s_ref[4] * wide, wide), wide)
    total = dot(a_ref[...], w_ref[first, :]) + dot(b_ref[...], w_ref[second, :])
    mixed = (tok_ref[...].astype(F32) + total).astype(BF)
    mixed_ref[...] = mixed
    yn_ref[...] = layer_norm(mixed.astype(F32)).astype(BF)


def gelu(v):
    return 0.5 * v * (1.0 + jnp.tanh((2.0 / jnp.pi) ** 0.5 * (v + 0.044715 * (v * v * v))))


def feed_kernel(parts, s_ref, yn_ref, *rest):
    sides = len(rest[:-1]) // parts
    out_ref = rest[-1]
    depth = rest[0].shape[1]
    starts = [pl.multiple_of(s_ref[5 + i] * depth, depth) for i in range(parts)]
    hidden = []
    for side in range(sides):
        bufs = rest[side * parts : (side + 1) * parts]
        total = sum(dot(yn_ref[:, pl.ds(starts[i], depth)], bufs[i][0]) for i in range(parts))
        hidden.append(gelu(total).astype(BF))
    for i in range(parts):
        total = sum(
            lax.dot_general(hidden[side], rest[side * parts + i][1], NT, preferred_element_type=F32)
            for side in range(sides)
        )
        out_ref[:, pl.ds(starts[i], depth)] = total.astype(out_ref.dtype)


def call(kernel, grid, in_specs, out_specs, out_shape, scratch=(), cost=(0, 0, 0)):
    return pl.pallas_call(
        kernel,
        grid_spec=pltpu.PrefetchScalarGridSpec(
            num_scalar_prefetch=1, grid=grid, in_specs=in_specs, out_specs=out_specs, scratch_shapes=scratch
        ),
        out_shape=out_shape,
        compiler_params=pltpu.CompilerParams(vmem_limit_bytes=VMEM_LIMIT),
        cost_estimate=pl.CostEstimate(flops=cost[0], bytes_accessed=cost[1], transcendentals=cost[2]),
    )


def shape(dims, dtype=BF):
    return jax.ShapeDtypeStruct(dims, dtype)


def whole(dims):
    return pl.BlockSpec(dims, lambda *_: (0,) * len(dims))


def after(x, *earlier):
    return lax.optimization_barrier((x,) + earlier)[0]


def on_device(layer_input, w_qkv, w_out, w_proj, w_up, w_down):
    tokens = layer_input[0]
    rows, width = tokens.shape
    heads, _, rank = w_proj.shape
    n, parts = lax.axis_size("seq"), lax.axis_size("dp")
    chips = n // 2
    me = lax.axis_index("seq")
    core = me % 2
    other = me + 1 - 2 * core
    inner = lambda i: ((i > 0) & (i < n - 1)).astype(jnp.int32)
    ring = [0] + list(range(1, parts, 2)) + list(range(2, parts, 2))[::-1]
    follow = [(ring[i], ring[(i + 1) % parts]) for i in range(parts)]
    dp = lax.axis_index("dp")
    held = [
        sum(jnp.where(dp == ring[i], ring[(i - s) % parts], 0) for i in range(parts)) for s in range(parts)
    ]
    scalars = jnp.stack([core, me // 2, inner(me), inner(other), 1 - core] + held).astype(jnp.int32)
    vmem = pl.BlockSpec(memory_space=pltpu.VMEM)

    swap = lambda x: lax.ppermute(x, "seq", [(i, i ^ 1) for i in range(n)])
    jump = lambda x, k: lax.ppermute(x, "seq", [(i, i ^ (2 * k)) for i in range(n)])
    edges = [(i, i + 1) for i in range(1, n - 1, 2)]

    partner = swap(tokens)
    halo = lax.ppermute(tokens, "seq", edges + [(j, i) for i, j in edges])

    own = jnp.stack([w_up, w_down])
    gathered = [own]

    def gather_part(s, *earlier):
        if s < parts:
            gathered.append(lax.ppermute(after(gathered[-1], *earlier), "dp", follow))

    gather_part(1)
    share = chips // 2
    shared = []

    def share_part(s, *earlier):
        if share and s < parts:
            shared.append(jump(after(gathered[s], *earlier) if earlier else gathered[s], share))

    share_part(0)
    hbm = lambda x: pltpu.with_memory_space_constraint(x, pltpu.HBM)
    w_qkv = hbm(w_qkv)

    half = heads // 2
    wide = half * HS
    block = 4 * HS
    steps = wide // block
    owned = half * rank // chips
    extra = max(16, 4 * owned // 128)
    blocks = width // block
    tok_spec = whole((rows, width))
    column = lambda which: pl.BlockSpec(
        (width, block), lambda g, s, which=which: (0, which * blocks + s[0] * steps + g)
    )
    proj_spec = pl.BlockSpec((4, HS, rank), lambda g, s: (s[0] * steps + g, 0, 0))
    slab = pl.BlockSpec((2 * rows, block), lambda g, s: (0, g))
    out = call(
        functools.partial(qkv_kernel, (chips, owned, extra, steps, rank)),
        (steps,),
        [tok_spec, tok_spec, column(0), column(1), column(2), proj_spec],
        [slab, slab, slab, whole((8, 128))] + [pl.BlockSpec(memory_space=pl.ANY)] * chips,
        [shape((2 * rows, wide))] * 3 + [shape((8, 128), F32)] + [shape((owned + extra, 128))] * chips,
        [
            pltpu.VMEM((2 * rows, width), BF),
            pltpu.VMEM((chips, owned + extra, 128), BF),
            pltpu.SemaphoreType.DMA((chips,)),
        ],
        (4 * rows * width * 3 * wide, 6 * width * wide, half * rank * 2 * rows),
    )(scalars, hbm(tokens), partner, w_qkv, w_qkv, w_qkv, hbm(w_proj))
    query, near_keys, near_values, top = out[:4]
    pays = [out[4]]
    for k in range(1, chips):
        pays.append(jump(out[4 + k], k))

    halo = after(halo, out[4])
    halo_partner = swap(halo)
    share_part(1, out[4])
    gather_part(2, out[4])
    per_head = pl.BlockSpec((2 * rows, 2 * block), lambda g, s: (0, g))
    near, peaks = call(
        near_kernel,
        (steps,),
        [whole((8, 128)), slab, slab, slab, tok_spec, tok_spec, column(1), column(2)],
        [per_head, whole((2 * rows, 128))],
        [shape((2 * rows, 2 * wide), F32), shape((2 * rows, 128), F32)],
        [pltpu.VMEM((2 * rows, width), BF)],
        (4 * rows * width * 2 * wide, 6 * width * wide, half * 3 * WBLK * 2 * rows),
    )(scalars, top, query, near_keys, near_values, halo, halo_partner, w_qkv, w_qkv)

    pays = [after(p, near) for p in pays]
    far = pl.pallas_call(
        functools.partial(combine_kernel, (chips, owned, extra)),
        out_shape=shape((owned, 128)),
        compiler_params=pltpu.CompilerParams(vmem_limit_bytes=VMEM_LIMIT),
        cost_estimate=pl.CostEstimate(flops=1000000, bytes_accessed=1000000, transcendentals=0),
    )(*pays)
    for s in range(3, parts):
        gather_part(s, far)
    share_part(2, far)
    fars = [far]
    for k in range(1, chips):
        fars.append(jump(far, k))
    mine, theirs = call(
        functools.partial(far_kernel, (chips, owned, rank)),
        (steps,),
        [whole((8, 128)), slab, per_head, whole((2 * rows, 128))] + [whole((owned, 128))] * chips,
        [pl.BlockSpec((rows, block), lambda g, s: (0, g))] * 2,
        [shape((rows, wide))] * 2,
        [pltpu.VMEM((half * rank, 128), BF)],
        (4 * rows * wide * rank * 2, 6 * rows * wide, half * rank * 2 * rows),
    )(scalars, top, query, near, peaks, *fars)
    arrived = swap(theirs)
    for s in range(3, parts):
        share_part(s, theirs)
    own_sides = gathered + [swap(after(w, theirs)) for w in gathered]
    mixed, yn = call(
        mix_kernel,
        (1,),
        [vmem] * 4,
        [vmem] * 2,
        [shape((rows, width))] * 2,
        (),
        (4 * rows * width * wide, 2 * width * width, 0),
    )(scalars, tokens, mine, arrived, w_out)


    def feed(x, dtype, weights):
        return call(
            functools.partial(feed_kernel, parts),
            (1,),
            [vmem] * (1 + len(weights)),
            vmem,
            shape((rows, width), dtype),
            (),
            (2 * rows * width * len(weights) * w_up.shape[1], len(weights) * own.size, rows * w_up.shape[1]),
        )(scalars, x, *weights)

    visits = range(1, max(share, 1))
    visitors = []
    for k in visits:
        visitors.append(jump(yn, k))
    terms = [feed(yn, F32, own_sides)]
    all_sides = own_sides
    if share:
        shared = [after(w, terms[0]) for w in shared]
        far_sides = shared + [swap(w) for w in shared]
        all_sides = own_sides + far_sides
    returned = []
    for k, x in zip(visits, visitors):
        x = feed(after(x, terms[0]), BF, all_sides)
        returned.append(jump(x, k))
    if share:
        terms.append(feed(after(yn, x) if returned else yn, F32, far_sides))
    result = mixed.astype(F32) + sum(terms)
    for x in returned:
        result = result + x.astype(F32)
    return result.astype(BF)[None]


def solution(mesh):
    in_specs = (P("dp", "seq", None), P(), P(), P(), P("dp", "seq"), P("dp", "seq"))
    out_specs = P("dp", "seq", None)
    return jax.shard_map(on_device, mesh=mesh, in_specs=in_specs, out_specs=out_specs, check_vma=False)
```

```python
import functools

import jax
import jax.numpy as jnp
from jax import lax
from jax.experimental import pallas as pl
from jax.experimental.pallas import tpu as pltpu
from jax.sharding import PartitionSpec as P


HS = 64
WBLK = 256
EPS = 1e-05
F32 = jnp.float32
BF = jnp.bfloat16
NT = (((1,), (1,)), ((), ()))
TT = (((0,), (1,)), ((), ()))
VMEM_LIMIT = 24 * 1024 * 1024
SMALL = 60.0


def dot(a, b):
    return jnp.dot(a, b, preferred_element_type=F32)


def layer_norm(x):
    center = x - jnp.mean(x, axis=-1, keepdims=True)
    spread = jnp.mean(center * center, axis=-1, keepdims=True)
    return center * lax.rsqrt(spread + EPS)


def head_average(width):
    a = lax.broadcasted_iota(jnp.int32, (width, width), 0) // HS
    b = lax.broadcasted_iota(jnp.int32, (width, width), 1) // HS
    return jnp.where(a == b, 1.0 / HS, 0.0).astype(F32)


def split(x):
    high = x.astype(BF)
    return high, (x - high.astype(F32)).astype(BF)


def blocks_of(x, size=256):
    return [x[:, i : i + size] for i in range(0, x.shape[1], size)]


def join(parts):
    return parts[0] if len(parts) == 1 else jnp.concatenate(parts, axis=1)


def head_norm(x):
    out, top = [], []
    for y in blocks_of(x):
        avg = head_average(y.shape[1]).astype(BF)
        mean = dot(y, avg)
        center = y.astype(F32) - mean
        spread = dot((center * center).astype(BF), avg)
        out.append((center * lax.rsqrt(spread + EPS)).astype(BF))
        top.append(spread + mean * mean)
    return join(out), functools.reduce(jnp.maximum, top)


def head_sum(x):
    out = []
    for y in blocks_of(x):
        square = y.astype(F32) * y.astype(F32)
        out.append(dot(square.astype(BF), head_average(y.shape[1]).astype(BF)) * HS)
    return functools.reduce(jnp.maximum, out)


def head_norm_wide(x):
    avg = head_average(x.shape[1]).astype(BF)

    def mean(y):
        one = y.astype(BF)
        rest = y - one.astype(F32)
        two, three = split(rest)
        return dot(one, avg) + dot(two, avg) + dot(three, avg)

    center = x - mean(x)
    spread = mean(center * center)
    return (center * lax.rsqrt(spread + EPS)).astype(BF)


def lanes(shape):
    return lax.broadcasted_iota(jnp.int32, shape, len(shape) - 1)


def diagonal(size):
    return lax.broadcasted_iota(jnp.int32, (size, size), 0) == lax.broadcasted_iota(
        jnp.int32, (size, size), 1
    )


def to_row(column):
    size = column.shape[0]
    return jnp.sum(jnp.where(diagonal(size), column, 0.0), axis=0, keepdims=True)


def to_column(row):
    size = row.shape[1]
    return jnp.sum(jnp.where(diagonal(size), row, 0.0), axis=1, keepdims=True)


def place_in_seq():
    me = lax.axis_index("seq")
    return lax.rem(me, 2), lax.div(me, 2)


def project_kernel(sizes, tok_hbm, par_ref, w_hbm, wp_hbm, q_ref, nk_ref, nv_ref, wk_ref, wv_ref, top_ref, *rest):
    chips, owned, _, rank = sizes
    pays, (tok_ref, wq_ref, wp_ref, xn_ref, kk_ref, vv_ref, pay_ref, stat_ref, sem, out_sem) = rest[:chips], rest[chips:]
    rows, width = tok_ref.shape
    wide = q_ref.shape[1]
    heads = wide // HS
    core, chip = place_in_seq()
    mine = lambda which: w_hbm.at[:, pl.ds(pl.multiple_of(which * width + core * wide, wide), wide)]
    loads = [
        pltpu.make_async_copy(tok_hbm, tok_ref, sem.at[0]),
        pltpu.make_async_copy(mine(1), wk_ref, sem.at[1]),
        pltpu.make_async_copy(mine(2), wv_ref, sem.at[2]),
        pltpu.make_async_copy(wp_hbm.at[pl.ds(core * heads, heads)], wp_ref, sem.at[3]),
        pltpu.make_async_copy(mine(0), wq_ref, sem.at[4]),
    ]
    for load in loads:
        load.start()
    xn_ref[rows:] = layer_norm(par_ref[...].astype(F32)).astype(BF)
    stat_ref[...] = jnp.zeros_like(stat_ref)
    loads[0].wait()
    xn_ref[:rows] = layer_norm(tok_ref[...].astype(F32)).astype(BF)
    x = xn_ref[...]
    loads[1].wait()
    kk = dot(x, wk_ref[...]).astype(BF)
    kk_ref[...] = kk
    loads[2].wait()
    vv = dot(x, wv_ref[...]).astype(BF)
    vv_ref[...] = vv
    loads[3].wait()
    nk_ref[...], key_top = head_norm(kk)
    nv_ref[...], _ = head_norm(vv)
    loads[4].wait()
    query = (dot(x, wq_ref[...]).astype(BF).astype(F32) * HS ** (-0.5)).astype(BF)
    q_ref[...] = query
    top_ref[...] = jnp.broadcast_to(jnp.max(head_sum(query)), top_ref.shape)
    stat_rows = owned // 128

    def pair_sums(pair, shifted):
        cut = pl.ds(pl.multiple_of(pair * 128, 128), 128)
        kp, vp = kk_ref[:, cut], vv_ref[:, cut]
        turned = pltpu.roll(vp.astype(F32), 64, 1).astype(BF)
        low_half = lanes(kp.shape) < HS
        for side in range(2):
            mixed = jnp.where(low_half, kp, turned) if side == 0 else jnp.where(low_half, turned, kp)
            wp = wp_ref[pair * 2 + side]
            none = jnp.zeros_like(wp)
            wide_wp = jnp.concatenate([wp, none] if side == 0 else [none, wp], axis=0)
            logits = lax.dot_general(wide_wp, kp, TT, preferred_element_type=F32)
            if shifted:
                peak = jnp.max(logits, axis=1, keepdims=True)
                logits = logits - peak
            weight = jnp.exp(logits).astype(BF)
            total = jnp.sum(weight.astype(F32), axis=1, keepdims=True)
            sums = dot(weight, mixed).astype(BF)
            for part in range(rank // 128):
                column = (pair * 2 + side) * rank + part * 128
                owner, offset = column // owned, column % owned
                here = slice(part * 128, (part + 1) * 128)
                pay_ref[owner, pl.ds(pl.multiple_of(offset, 128), 128), :] = sums[here]
                entries = [(3, to_row(total[here]))]
                if shifted:
                    one = to_row(peak[here])
                    first = one.astype(BF).astype(F32)
                    second = (one - first).astype(BF).astype(F32)
                    entries += [(0, first), (1, second), (2, one - first - second)]
                for i, row in entries:
                    stat_ref[owner, pl.ds(i * stat_rows + offset // 128, 1), :] = row

    column_norm = jnp.max(jnp.sum(jnp.square(wp_ref[...].astype(F32)), axis=1))
    near_zero = jnp.max(key_top) * HS * column_norm < SMALL * SMALL

    @pl.when(near_zero)
    def _():
        for pair in range(heads // 2):
            pair_sums(pair, False)

    @pl.when(jnp.logical_not(near_zero))
    def _():
        def one(pair, carry):
            pair_sums(pair, True)
            return carry

        lax.fori_loop(0, heads // 2, one, 0)

    pay_ref[:, owned:, :] = stat_ref[...].astype(BF)
    copies = [
        pltpu.make_async_copy(pay_ref.at[lax.bitwise_xor(chip, k)], pays[k], out_sem.at[k]) for k in range(chips)
    ]
    for copy in copies:
        copy.start()
    for copy in copies:
        copy.wait()


def combine_kernel(sizes, *refs):
    chips, owned, extra = sizes
    pays, far_ref = refs[:chips], refs[chips]
    stat_rows = owned // 128
    tails = [p[owned : owned + extra, :].astype(F32) for p in pays]
    peaks = [
        t[:stat_rows] + t[stat_rows : 2 * stat_rows] + t[2 * stat_rows : 3 * stat_rows] for t in tails
    ]
    peak = functools.reduce(jnp.maximum, peaks)
    scales = [jnp.exp(p - peak) for p in peaks]
    total = sum(s * t[3 * stat_rows : 4 * stat_rows] for s, t in zip(scales, tails))
    scales = [s / total for s in scales]
    for i in range(stat_rows):
        cut = slice(i * 128, (i + 1) * 128)
        summary = sum(to_column(s[i : i + 1]) * p[cut, :].astype(F32) for s, p in zip(scales, pays))
        far_ref[cut, :] = head_norm_wide(summary)


def one_head(qp, side):
    low_half = lanes(qp.shape) < HS
    none = jnp.zeros_like(qp)
    return jnp.where(low_half, qp, none) if side == 0 else jnp.where(low_half, none, qp)


def with_ones(v, side):
    low_half = lanes(v.shape) < HS
    ones = jnp.ones_like(v)
    return jnp.where(low_half, v, ones) if side == 0 else jnp.where(low_half, ones, v)


def small_scores(top_ref):
    return jnp.max(top_ref[...]) * (HS * 1.02) < SMALL * SMALL


def near_kernel(group, top_ref, q_ref, nk_ref, nv_ref, *rest):
    if group == 0:
        halo_ref, halop_ref, wk_ref, wv_ref, o_ref, m_ref, hk_ref, hv_ref, xh_ref = rest
        half = halo_ref.shape[0]
        xh_ref[:half] = layer_norm(halo_ref[...].astype(F32)).astype(BF)
        xh_ref[half:] = layer_norm(halop_ref[...].astype(F32)).astype(BF)
        x = xh_ref[...]
        hk_ref[...], _ = head_norm(dot(x, wk_ref[...]).astype(BF))
        hv_ref[...], _ = head_norm(dot(x, wv_ref[...]).astype(BF))
    else:
        hk_ref, hv_ref, o_ref, m_ref = rest
    rows = hk_ref.shape[0] // 2
    heads = o_ref.shape[1] // 128
    me, n = lax.axis_index("seq"), lax.axis_size("seq")
    other = lax.bitwise_xor(me, 1)
    inside = [(i > 0) & (i < n - 1) for i in (me, other)]
    place = lanes((rows, 128))

    def attend(pair, shifted):
        cut = pl.ds(pl.multiple_of(group * heads * HS + pair * 128, 128), 128)
        kp = nk_ref[:, cut]
        for side in range(2):
            head = pair * 2 + side
            vp = with_ones(nv_ref[:, cut], side)
            for part in range(2):
                these = slice(part * rows, (part + 1) * rows)
                qm = one_head(q_ref[these, cut], side)
                main = lax.dot_general(qm, kp, NT, preferred_element_type=F32)
                halo = lax.dot_general(qm, hk_ref[these, cut], NT, preferred_element_type=F32)
                halo = halo + jnp.where(inside[part], 0.0, -jnp.inf).astype(F32)
                if shifted:
                    peak = jnp.maximum(
                        jnp.max(main, axis=1, keepdims=True), jnp.max(halo, axis=1, keepdims=True)
                    )
                    main, halo = main - peak, halo - peak
                    m_ref[these] = jnp.where(place == head, peak, m_ref[these])
                out = dot(jnp.exp(main).astype(BF), vp)
                out = out + dot(jnp.exp(halo).astype(BF), with_ones(hv_ref[these, cut], side))
                o_ref[these, pl.ds(pl.multiple_of(head * 128, 128), 128)] = out

    small = small_scores(top_ref)
    m_ref[...] = jnp.zeros_like(m_ref)

    @pl.when(small)
    def _():
        for pair in range(heads // 2):
            attend(pair, False)

    @pl.when(jnp.logical_not(small))
    def _():
        def one(pair, carry):
            attend(pair, True)
            return carry

        lax.fori_loop(0, heads // 2, one, 0)


def far_kernel(sizes, top_ref, q_ref, o_ref, m_ref, *rest):
    chips, owned, rank, group = sizes
    fars, (mine_ref, theirs_ref, all_ref) = rest[:chips], rest[chips:]
    rows = mine_ref.shape[0]
    heads = o_ref.shape[1] // 128
    _, chip = place_in_seq()
    for k in range(chips):
        source = lax.bitwise_xor(chip, k)
        all_ref[pl.ds(pl.multiple_of(source * owned, owned), owned), :] = fars[k][...]
    place = lanes((rows, 128))

    def attend(pair, shifted):
        cut = pl.ds(pl.multiple_of(group * heads * HS + pair * 128, 128), 128)
        low_half = lanes((rows, 128)) < HS
        for part in range(2):
            these = slice(part * rows, (part + 1) * rows)
            sums = []
            for side in range(2):
                qm = one_head(q_ref[these, cut], side)
                head = pair * 2 + side
                kv = all_ref[pl.ds(pl.multiple_of((group * heads + head) * rank, rank), rank), :]
                scores = lax.dot_general(qm, kv, NT, preferred_element_type=F32)
                before = o_ref[these, pl.ds(pl.multiple_of(head * 128, 128), 128)]
                if shifted:
                    peak = jnp.sum(jnp.where(place == head, m_ref[these], 0.0), axis=1, keepdims=True)
                    new = jnp.maximum(peak, jnp.max(scores, axis=1, keepdims=True))
                    scores = scores - new
                    before = before * jnp.exp(peak - new)
                out = dot(jnp.exp(scores).astype(BF), with_ones(kv, 1 - side))
                sums.append(before + pltpu.roll(out, 64, 1))
            total = pltpu.roll(jnp.where(low_half, sums[1], sums[0]), 64, 1)
            result = (jnp.where(low_half, sums[0], sums[1]) / total).astype(BF)
            (mine_ref, theirs_ref)[part][:, pl.ds(pl.multiple_of(pair * 128, 128), 128)] = result

    small = small_scores(top_ref)

    @pl.when(small)
    def _():
        for pair in range(heads // 2):
            attend(pair, False)

    @pl.when(jnp.logical_not(small))
    def _():
        def one(pair, carry):
            attend(pair, True)
            return carry

        lax.fori_loop(0, heads // 2, one, 0)


def mix_kernel(tok_ref, *rest):
    pieces, (w_ref, mixed_ref, yn_ref) = rest[:-3], rest[-3:]
    wide = pieces[0].shape[1]
    half = len(pieces) // 2
    total = 0.0
    core, _ = place_in_seq()
    for i, piece in enumerate(pieces):
        owner = core if i < half else 1 - core
        start = pl.multiple_of((owner * half + i % half) * wide, wide)
        total = total + dot(piece[...], w_ref[pl.ds(start, wide), :])
    mixed = (tok_ref[...].astype(F32) + total).astype(BF)
    mixed_ref[...] = mixed
    yn_ref[...] = layer_norm(mixed.astype(F32)).astype(BF)


def gelu(v):
    return 0.5 * v * (1.0 + jnp.tanh((2.0 / jnp.pi) ** 0.5 * (v + 0.044715 * (v * v * v))))


def folded(size):
    return [0] + list(range(1, size, 2)) + list(range(2, size, 2))[::-1]


def feed_kernel(parts, yn_ref, *rest):
    sides = len(rest[:-1]) // parts
    out_ref = rest[-1]
    depth = rest[0].shape[1]
    dp = lax.axis_index("dp")
    ring = folded(parts)
    starts = []
    for s in range(parts):
        block = sum(jnp.where(dp == ring[i], ring[(i - s) % parts], 0) for i in range(parts))
        starts.append(pl.multiple_of(block * depth, depth))
    hidden = []
    for side in range(sides):
        bufs = rest[side * parts : (side + 1) * parts]
        total = sum(dot(yn_ref[:, pl.ds(starts[i], depth)], bufs[i][0]) for i in range(parts))
        hidden.append(gelu(total).astype(BF))
    for i in range(parts):
        total = sum(
            lax.dot_general(hidden[side], rest[side * parts + i][1], NT, preferred_element_type=F32)
            for side in range(sides)
        )
        out_ref[:, pl.ds(starts[i], depth)] = total.astype(out_ref.dtype)


def call(kernel, in_specs, out_specs, out_shape, scratch=(), cost=(0, 0, 0)):
    return pl.pallas_call(
        kernel,
        in_specs=in_specs,
        out_specs=out_specs,
        scratch_shapes=scratch,
        out_shape=out_shape,
        compiler_params=pltpu.CompilerParams(vmem_limit_bytes=VMEM_LIMIT),
        cost_estimate=pl.CostEstimate(flops=cost[0], bytes_accessed=cost[1], transcendentals=cost[2]),
    )


def shape(dims, dtype=BF):
    return jax.ShapeDtypeStruct(dims, dtype)


def after(x, *earlier):
    return lax.optimization_barrier((x,) + earlier)[0]


def on_device(layer_input, w_qkv, w_out, w_proj, w_up, w_down):
    tokens = layer_input[0]
    rows, width = tokens.shape
    heads, _, rank = w_proj.shape
    n, parts = lax.axis_size("seq"), lax.axis_size("dp")
    chips = n // 2
    ring = folded(parts)
    follow = [(ring[i], ring[(i + 1) % parts]) for i in range(parts)]
    anywhere = pl.BlockSpec(memory_space=pl.ANY)
    hbm = lambda x: pltpu.with_memory_space_constraint(x, pltpu.HBM)
    vmem = pl.BlockSpec(memory_space=pltpu.VMEM)

    swap = lambda x: lax.ppermute(x, "seq", [(i, i ^ 1) for i in range(n)])
    jump = lambda x, k: lax.ppermute(x, "seq", [(i, i ^ (2 * k)) for i in range(n)])
    cross = lambda x, ks: lax.ppermute(x, "seq", [(i, i ^ (2 * ks[i % 2])) for i in range(n)])
    edges = [(i, i + 1) for i in range(1, n - 1, 2)]

    partner = swap(tokens)
    halo = lax.ppermute(tokens, "seq", edges + [(j, i) for i, j in edges])

    own = jnp.stack([w_up, w_down])
    gathered = [own]

    def gather_part(s, *earlier):
        if s < parts:
            gathered.append(lax.ppermute(after(gathered[-1], *earlier), "dp", follow))

    gather_part(1)
    share = (chips // 2, 1) if chips > 1 else ()
    shared = []

    def share_part(s, *earlier):
        if share and s < parts:
            shared.append(cross(after(gathered[s], *earlier) if earlier else gathered[s], share))

    share_part(0)

    half = heads // 2
    wide = half * HS
    block = 4 * HS
    steps = wide // block
    owned = half * rank // chips
    extra = max(16, 4 * owned // 128)
    hbm_space = pl.BlockSpec(memory_space=pltpu.HBM)
    out = call(
        functools.partial(project_kernel, (chips, owned, extra, rank)),
        [hbm_space, vmem, hbm_space, hbm_space],
        [vmem] * 6 + [anywhere] * chips,
        [shape((2 * rows, wide))] * 3
        + [shape((width, wide))] * 2
        + [shape((8, 128), F32)]
        + [shape((owned + extra, 128))] * chips,
        [
            pltpu.VMEM((rows, width), BF),
            pltpu.VMEM((width, wide), BF),
            pltpu.VMEM((half, HS, rank), BF),
            pltpu.VMEM((2 * rows, width), BF),
            pltpu.VMEM((2 * rows, wide), BF),
            pltpu.VMEM((2 * rows, wide), BF),
            pltpu.VMEM((chips, owned + extra, 128), BF),
            pltpu.VMEM((chips, extra, 128), F32),
            pltpu.SemaphoreType.DMA((5,)),
            pltpu.SemaphoreType.DMA((chips,)),
        ],
        (4 * rows * width * 3 * wide, 6 * width * wide, half * rank * 2 * rows),
    )(hbm(tokens), partner, hbm(w_qkv), hbm(w_proj))
    query, near_keys, near_values, w_key, w_value, top = out[:6]
    out = out[6:]
    pays = [out[0]]
    for k in range(1, chips):
        pays.append(jump(out[k], k))

    halo = after(halo, top)
    halo_partner = swap(halo)
    share_part(1, top)
    gather_part(2, top)
    halos, near = [halo, halo_partner, w_key, w_value], []

    def near_part(g, *earlier):
        kept = [shape((2 * rows, wide))] * 2 if g == 0 else []
        res = call(
            functools.partial(near_kernel, g),
            [vmem] * (4 + len(halos)),
            [vmem] * (2 + len(kept)),
            [shape((2 * rows, 2 * block), F32), shape((2 * rows, 128), F32)] + kept,
            [pltpu.VMEM((2 * rows, width), BF)] if g == 0 else [],
            (4 * rows * width * 2 * block, 4 * width * block, 4 * 3 * WBLK * 2 * rows),
        )(after(top, *earlier) if earlier else top, query, near_keys, near_values, *halos)
        near.append(res[:2])
        return res[2:]

    halos = near_part(0)
    pays = [after(p, near[0][0]) for p in pays]
    far = pl.pallas_call(
        functools.partial(combine_kernel, (chips, owned, extra)),
        out_shape=shape((owned, 128)),
        compiler_params=pltpu.CompilerParams(vmem_limit_bytes=VMEM_LIMIT),
        cost_estimate=pl.CostEstimate(flops=1000000, bytes_accessed=1000000, transcendentals=0),
    )(*pays)
    share_part(2, far)
    for s in range(3, parts):
        gather_part(s, far)
    fars = [far]
    for k in range(1, chips):
        fars.append(jump(far, k))
    for g in range(1, steps):
        near_part(g, far)
    fars = [after(x, near[-1][0]) for x in fars]
    pieces = []
    for g in range(steps):
        pieces.append(
            call(
                functools.partial(far_kernel, (chips, owned, rank, g)),
                [vmem] * (4 + chips),
                [vmem] * 2,
                [shape((rows, block))] * 2,
                [pltpu.VMEM((half * rank, 128), BF)],
                (4 * rows * block * rank * 2, 6 * rows * block, 4 * rank * 2 * rows),
            )(top, query, *near[g], *fars)
        )
    arrived = []
    for g in range(steps):
        arrived.append(swap(pieces[g][1]))
    theirs = pieces[-1][1]
    mixed, yn = call(
        mix_kernel,
        [vmem] * (2 + 2 * steps),
        [vmem] * 2,
        [shape((rows, width))] * 2,
        (),
        (4 * rows * width * wide, 2 * width * width, 0),
    )(tokens, *[piece[0] for piece in pieces], *arrived, w_out)
    for s in range(3, parts):
        share_part(s, yn)
    own_sides = list(gathered)
    for w in gathered:
        own_sides.append(swap(after(w, theirs)))

    def feed(x, dtype, weights):
        return call(
            functools.partial(feed_kernel, parts),
            [vmem] * (1 + len(weights)),
            vmem,
            shape((rows, width), dtype),
            (),
            (2 * rows * width * len(weights) * w_up.shape[1], len(weights) * own.size, rows * w_up.shape[1]),
        )(x, *weights)

    routes = list(zip(*[[k for k in range(1, chips) if not k & bit] for bit in share]))
    visitors = []
    for ks in routes:
        for which, route in enumerate((ks, ks[::-1])):
            visitors.append((which, route, cross(yn, route)))
    terms = [feed(yn, F32, own_sides)]
    mine_sides, their_sides = list(gathered), own_sides[parts:]
    if share:
        swapped = []
        for i, w in enumerate(shared):
            swapped.append(swap(after(w, theirs if i < 2 else terms[0])))
        mine_sides += shared
        their_sides = their_sides + swapped
    returned, last = [], yn
    for which, route, x in visitors:
        last = feed(after(x, terms[0]), BF, (mine_sides, their_sides)[which])
        returned.append(cross(last, route))
    if share:
        terms.append(feed(after(yn, last), F32, mine_sides[parts:] + their_sides[parts:]))
    result = mixed.astype(F32) + sum(terms)
    for x in returned:
        result = result + x.astype(F32)
    return result.astype(BF)[None]


def solution(mesh):
    in_specs = (P("dp", "seq", None), P(), P(), P(), P("dp", "seq"), P("dp", "seq"))
    out_specs = P("dp", "seq", None)
    return jax.shard_map(
        on_device, mesh=mesh, in_specs=in_specs, out_specs=out_specs, check_vma=False
    )
```

```python
import functools

import jax
import jax.numpy as jnp
from jax import lax
from jax.experimental import pallas as pl
from jax.experimental.pallas import tpu as pltpu
from jax.sharding import PartitionSpec as P


HS = 64
EPS = 1e-05
F32 = jnp.float32
BF = jnp.bfloat16
NT = (((1,), (1,)), ((), ()))
TT = (((0,), (1,)), ((), ()))
VMEM_LIMIT = 24 * 1024 * 1024
SMALL = 60.0
CUTS = 2


def dot(a, b):
    return jnp.dot(a, b, preferred_element_type=F32)


def layer_norm(x):
    center = x - jnp.mean(x, axis=-1, keepdims=True)
    spread = jnp.mean(center * center, axis=-1, keepdims=True)
    return center * lax.rsqrt(spread + EPS)


def head_average(width):
    a = lax.broadcasted_iota(jnp.int32, (width, width), 0) // HS
    b = lax.broadcasted_iota(jnp.int32, (width, width), 1) // HS
    return jnp.where(a == b, 1.0 / HS, 0.0).astype(F32)


def split(x):
    high = x.astype(BF)
    return high, (x - high.astype(F32)).astype(BF)


def blocks_of(x, size=256):
    return [x[:, i : i + size] for i in range(0, x.shape[1], size)]


def join(parts):
    return parts[0] if len(parts) == 1 else jnp.concatenate(parts, axis=1)


def head_norm(x):
    out, top = [], []
    for y in blocks_of(x):
        avg = head_average(y.shape[1]).astype(BF)
        mean = dot(y, avg)
        center = y.astype(F32) - mean
        spread = dot((center * center).astype(BF), avg)
        out.append((center * lax.rsqrt(spread + EPS)).astype(BF))
        top.append(spread + mean * mean)
    return join(out), functools.reduce(jnp.maximum, top)


def head_sum(x):
    out = []
    for y in blocks_of(x):
        square = y.astype(F32) * y.astype(F32)
        out.append(dot(square.astype(BF), head_average(y.shape[1]).astype(BF)) * HS)
    return functools.reduce(jnp.maximum, out)


def head_norm_wide(x):
    avg = head_average(x.shape[1]).astype(BF)

    def mean(y):
        one = y.astype(BF)
        rest = y - one.astype(F32)
        two, three = split(rest)
        return dot(one, avg) + dot(two, avg) + dot(three, avg)

    center = x - mean(x)
    spread = mean(center * center)
    return (center * lax.rsqrt(spread + EPS)).astype(BF)


def lanes(shape):
    return lax.broadcasted_iota(jnp.int32, shape, len(shape) - 1)


def diagonal(size):
    return lax.broadcasted_iota(jnp.int32, (size, size), 0) == lax.broadcasted_iota(
        jnp.int32, (size, size), 1
    )


def to_row(column):
    size = column.shape[0]
    return jnp.sum(jnp.where(diagonal(size), column, 0.0), axis=0, keepdims=True)


def to_column(row):
    size = row.shape[1]
    return jnp.sum(jnp.where(diagonal(size), row, 0.0), axis=1, keepdims=True)


def place_in_seq():
    me = lax.axis_index("seq")
    return lax.rem(me, 2), lax.div(me, 2)


def project_kernel(sizes, tok_hbm, par_ref, w_hbm, wp_hbm, q_ref, nk_ref, nv_ref, wk_ref, wv_ref, top_ref, *rest):
    chips, owned, _, rank = sizes
    pays, (tok_ref, wq_ref, wp_ref, xn_ref, kk_ref, vv_ref, pay_ref, stat_ref, sem, out_sem) = rest[:chips], rest[chips:]
    rows, width = tok_ref.shape
    wide = q_ref.shape[1]
    heads = wide // HS
    core, chip = place_in_seq()
    mine = lambda which: w_hbm.at[:, pl.ds(pl.multiple_of(which * width + core * wide, wide), wide)]
    loads = [
        pltpu.make_async_copy(tok_hbm, tok_ref, sem.at[0]),
        pltpu.make_async_copy(mine(1), wk_ref, sem.at[1]),
        pltpu.make_async_copy(mine(2), wv_ref, sem.at[2]),
        pltpu.make_async_copy(wp_hbm.at[pl.ds(core * heads, heads)], wp_ref, sem.at[3]),
        pltpu.make_async_copy(mine(0), wq_ref, sem.at[4]),
    ]
    for load in loads:
        load.start()
    xn_ref[rows:] = layer_norm(par_ref[...].astype(F32)).astype(BF)
    stat_ref[...] = jnp.zeros_like(stat_ref)
    loads[0].wait()
    xn_ref[:rows] = layer_norm(tok_ref[...].astype(F32)).astype(BF)
    x = xn_ref[...]
    loads[1].wait()
    kk = dot(x, wk_ref[...]).astype(BF)
    kk_ref[...] = kk
    loads[2].wait()
    vv = dot(x, wv_ref[...]).astype(BF)
    vv_ref[...] = vv
    loads[3].wait()
    nk_ref[...], key_top = head_norm(kk)
    nv_ref[...], _ = head_norm(vv)
    loads[4].wait()
    query = (dot(x, wq_ref[...]).astype(BF).astype(F32) * HS ** (-0.5)).astype(BF)
    q_ref[...] = query
    top_ref[...] = jnp.broadcast_to(jnp.max(head_sum(query)), top_ref.shape)
    stat_rows = owned // 128

    def pair_sums(pair, shifted):
        cut = pl.ds(pl.multiple_of(pair * 128, 128), 128)
        kp, vp = kk_ref[:, cut], vv_ref[:, cut]
        turned = pltpu.roll(vp.astype(F32), 64, 1).astype(BF)
        low_half = lanes(kp.shape) < HS
        for side in range(2):
            mixed = jnp.where(low_half, kp, turned) if side == 0 else jnp.where(low_half, turned, kp)
            wp = wp_ref[pair * 2 + side]
            none = jnp.zeros_like(wp)
            wide_wp = jnp.concatenate([wp, none] if side == 0 else [none, wp], axis=0)
            logits = lax.dot_general(wide_wp, kp, TT, preferred_element_type=F32)
            if shifted:
                peak = jnp.max(logits, axis=1, keepdims=True)
                logits = logits - peak
            weight = jnp.exp(logits).astype(BF)
            total = jnp.sum(weight.astype(F32), axis=1, keepdims=True)
            sums = dot(weight, mixed).astype(BF)
            for part in range(rank // 128):
                column = (pair * 2 + side) * rank + part * 128
                owner, offset = column // owned, column % owned
                here = slice(part * 128, (part + 1) * 128)
                pay_ref[owner, pl.ds(pl.multiple_of(offset, 128), 128), :] = sums[here]
                entries = [(3, to_row(total[here]))]
                if shifted:
                    one = to_row(peak[here])
                    first = one.astype(BF).astype(F32)
                    second = (one - first).astype(BF).astype(F32)
                    entries += [(0, first), (1, second), (2, one - first - second)]
                for i, row in entries:
                    stat_ref[owner, pl.ds(i * stat_rows + offset // 128, 1), :] = row

    column_norm = jnp.max(jnp.sum(jnp.square(wp_ref[...].astype(F32)), axis=1))
    near_zero = jnp.max(key_top) * HS * column_norm < SMALL * SMALL

    @pl.when(near_zero)
    def _():
        for pair in range(heads // 2):
            pair_sums(pair, False)

    @pl.when(jnp.logical_not(near_zero))
    def _():
        def one(pair, carry):
            pair_sums(pair, True)
            return carry

        lax.fori_loop(0, heads // 2, one, 0)

    pay_ref[:, owned:, :] = stat_ref[...].astype(BF)
    copies = [
        pltpu.make_async_copy(pay_ref.at[lax.bitwise_xor(chip, k)], pays[k], out_sem.at[k]) for k in range(chips)
    ]
    for copy in copies:
        copy.start()
    for copy in copies:
        copy.wait()


def combine_kernel(sizes, *refs):
    chips, owned, extra = sizes
    pays, far_ref = refs[:chips], refs[chips]
    stat_rows = owned // 128
    tails = [p[owned : owned + extra, :].astype(F32) for p in pays]
    peaks = [
        t[:stat_rows] + t[stat_rows : 2 * stat_rows] + t[2 * stat_rows : 3 * stat_rows] for t in tails
    ]
    peak = functools.reduce(jnp.maximum, peaks)
    scales = [jnp.exp(p - peak) for p in peaks]
    total = sum(s * t[3 * stat_rows : 4 * stat_rows] for s, t in zip(scales, tails))
    scales = [s / total for s in scales]
    for i in range(stat_rows):
        cut = slice(i * 128, (i + 1) * 128)
        summary = sum(to_column(s[i : i + 1]) * p[cut, :].astype(F32) for s, p in zip(scales, pays))
        far_ref[cut, :] = head_norm_wide(summary)


def one_head(qp, side):
    low_half = lanes(qp.shape) < HS
    none = jnp.zeros_like(qp)
    return jnp.where(low_half, qp, none) if side == 0 else jnp.where(low_half, none, qp)


def with_ones(v, side):
    low_half = lanes(v.shape) < HS
    ones = jnp.ones_like(v)
    return jnp.where(low_half, v, ones) if side == 0 else jnp.where(low_half, ones, v)


def small_scores(top_ref):
    return jnp.max(top_ref[...]) * (HS * 1.02) < SMALL * SMALL


def both_ways(small, heads, attend):
    @pl.when(small)
    def _():
        for pair in range(heads // 2):
            attend(pair, False)

    @pl.when(jnp.logical_not(small))
    def _():
        def one(pair, carry):
            attend(pair, True)
            return carry

        lax.fori_loop(0, heads // 2, one, 0)


def pair_cut(pair):
    return pl.ds(pl.multiple_of(pair * 128, 128), 128)


def near_kernel(top_ref, q_ref, nk_ref, nv_ref, o_ref, m_ref):
    rows = q_ref.shape[0] // 2
    place = lanes((rows, 128))
    m_ref[...] = jnp.zeros_like(m_ref)

    def attend(pair, shifted):
        cut = pair_cut(pair)
        kp = nk_ref[:, cut]
        for side in range(2):
            vp = with_ones(nv_ref[:, cut], side)
            for part in range(2):
                these = slice(part * rows, (part + 1) * rows)
                qm = one_head(q_ref[these, cut], side)
                scores = lax.dot_general(qm, kp, NT, preferred_element_type=F32)
                if shifted:
                    peak = jnp.max(scores, axis=1, keepdims=True)
                    scores = scores - peak
                    m_ref[these] = jnp.where(place == pair * 2 + side, peak, m_ref[these])
                o_ref[these, pair_cut(pair * 2 + side)] = dot(jnp.exp(scores).astype(BF), vp)

    both_ways(small_scores(top_ref), nk_ref.shape[1] // HS, attend)


def halo_kernel(top_ref, q_ref, before_ref, mb_ref, halo_ref, halop_ref, wk_ref, wv_ref, o_ref, m_ref, xh_ref, hk_ref, hv_ref):
    rows = halo_ref.shape[0]
    xh_ref[:rows] = layer_norm(halo_ref[...].astype(F32)).astype(BF)
    xh_ref[rows:] = layer_norm(halop_ref[...].astype(F32)).astype(BF)
    x = xh_ref[...]
    hk_ref[...], _ = head_norm(dot(x, wk_ref[...]).astype(BF))
    hv_ref[...], _ = head_norm(dot(x, wv_ref[...]).astype(BF))
    me, n = lax.axis_index("seq"), lax.axis_size("seq")
    other = lax.bitwise_xor(me, 1)
    inside = [(i > 0) & (i < n - 1) for i in (me, other)]
    place = lanes((rows, 128))
    m_ref[...] = mb_ref[...]

    def attend(pair, shifted):
        cut = pair_cut(pair)
        for side in range(2):
            here = pair_cut(pair * 2 + side)
            for part in range(2):
                these = slice(part * rows, (part + 1) * rows)
                qm = one_head(q_ref[these, cut], side)
                scores = lax.dot_general(qm, hk_ref[these, cut], NT, preferred_element_type=F32)
                scores = scores + jnp.where(inside[part], 0.0, -jnp.inf).astype(F32)
                before = before_ref[these, here]
                if shifted:
                    head = place == pair * 2 + side
                    peak = jnp.sum(jnp.where(head, mb_ref[these], 0.0), axis=1, keepdims=True)
                    new = jnp.maximum(peak, jnp.max(scores, axis=1, keepdims=True))
                    scores = scores - new
                    before = before * jnp.exp(peak - new)
                    m_ref[these] = jnp.where(head, new, m_ref[these])
                o_ref[these, here] = before + dot(jnp.exp(scores).astype(BF), with_ones(hv_ref[these, cut], side))

    both_ways(small_scores(top_ref), hk_ref.shape[1] // HS, attend)


def far_kernel(sizes, top_ref, q_ref, o_ref, m_ref, *rest):
    chips, owned, rank, group = sizes
    fars, (mine_ref, theirs_ref, all_ref) = rest[:chips], rest[chips:]
    rows = mine_ref.shape[0]
    heads = mine_ref.shape[1] // HS
    _, chip = place_in_seq()
    for k in range(chips):
        source = lax.bitwise_xor(chip, k)
        all_ref[pl.ds(pl.multiple_of(source * owned, owned), owned), :] = fars[k][...]
    place = lanes((rows, 128))

    def attend(pair, shifted):
        whole_pair = group * (heads // 2) + pair
        cut = pair_cut(whole_pair)
        low_half = lanes((rows, 128)) < HS
        for part in range(2):
            these = slice(part * rows, (part + 1) * rows)
            sums = []
            for side in range(2):
                qm = one_head(q_ref[these, cut], side)
                head = whole_pair * 2 + side
                kv = all_ref[pl.ds(pl.multiple_of(head * rank, rank), rank), :]
                scores = lax.dot_general(qm, kv, NT, preferred_element_type=F32)
                before = o_ref[these, pair_cut(head)]
                if shifted:
                    peak = jnp.sum(jnp.where(place == head, m_ref[these], 0.0), axis=1, keepdims=True)
                    new = jnp.maximum(peak, jnp.max(scores, axis=1, keepdims=True))
                    scores = scores - new
                    before = before * jnp.exp(peak - new)
                out = dot(jnp.exp(scores).astype(BF), with_ones(kv, 1 - side))
                sums.append(before + pltpu.roll(out, 64, 1))
            total = pltpu.roll(jnp.where(low_half, sums[1], sums[0]), 64, 1)
            result = (jnp.where(low_half, sums[0], sums[1]) / total).astype(BF)
            (mine_ref, theirs_ref)[part][:, pair_cut(pair)] = result

    both_ways(small_scores(top_ref), heads, attend)


def mix_kernel(cuts, tok_ref, *rest):
    rest, cut_refs = rest[:-cuts], rest[-cuts:]
    pieces, (w_ref, mixed_ref, yn_ref) = rest[:-3], rest[-3:]
    wide = pieces[0].shape[1]
    half = len(pieces) // 2
    total = 0.0
    core, _ = place_in_seq()
    for i, piece in enumerate(pieces):
        owner = core if i < half else 1 - core
        start = pl.multiple_of((owner * half + i % half) * wide, wide)
        total = total + dot(piece[...], w_ref[pl.ds(start, wide), :])
    mixed = (tok_ref[...].astype(F32) + total).astype(BF)
    mixed_ref[...] = mixed
    yn = layer_norm(mixed.astype(F32)).astype(BF)
    yn_ref[...] = yn
    size = yn.shape[0] // cuts
    for i, cut_ref in enumerate(cut_refs):
        cut_ref[...] = yn[i * size : (i + 1) * size]


def gelu(v):
    return 0.5 * v * (1.0 + jnp.tanh((2.0 / jnp.pi) ** 0.5 * (v + 0.044715 * (v * v * v))))


def folded(size):
    return [0] + list(range(1, size, 2)) + list(range(2, size, 2))[::-1]


def feed_kernel(parts, added, yn_ref, *rest):
    rest, more, out_ref = rest[: -1 - added], rest[-1 - added : -1], rest[-1]
    sides = len(rest) // parts
    depth = rest[0].shape[1]
    dp = lax.axis_index("dp")
    ring = folded(parts)
    starts = []
    for s in range(parts):
        block = sum(jnp.where(dp == ring[i], ring[(i - s) % parts], 0) for i in range(parts))
        starts.append(pl.multiple_of(block * depth, depth))
    hidden = []
    for side in range(sides):
        bufs = rest[side * parts : (side + 1) * parts]
        total = sum(dot(yn_ref[:, pl.ds(starts[i], depth)], bufs[i][0]) for i in range(parts))
        hidden.append(gelu(total).astype(BF))
    for i in range(parts):
        total = sum(
            lax.dot_general(hidden[side], rest[side * parts + i][1], NT, preferred_element_type=F32)
            for side in range(sides)
        )
        for ref in more:
            total = total + ref[:, pl.ds(starts[i], depth)].astype(F32)
        out_ref[:, pl.ds(starts[i], depth)] = total.astype(out_ref.dtype)


def call(kernel, in_specs, out_specs, out_shape, scratch=(), cost=(0, 0, 0)):
    return pl.pallas_call(
        kernel,
        in_specs=in_specs,
        out_specs=out_specs,
        scratch_shapes=scratch,
        out_shape=out_shape,
        compiler_params=pltpu.CompilerParams(vmem_limit_bytes=VMEM_LIMIT),
        cost_estimate=pl.CostEstimate(flops=cost[0], bytes_accessed=cost[1], transcendentals=cost[2]),
    )


def shape(dims, dtype=BF):
    return jax.ShapeDtypeStruct(dims, dtype)


def after(x, *earlier):
    return lax.optimization_barrier((x,) + earlier)[0]


def on_device(layer_input, w_qkv, w_out, w_proj, w_up, w_down):
    tokens = layer_input[0]
    rows, width = tokens.shape
    heads, _, rank = w_proj.shape
    n, parts = lax.axis_size("seq"), lax.axis_size("dp")
    chips = n // 2
    ring = folded(parts)
    follow = [(ring[i], ring[(i + 1) % parts]) for i in range(parts)]
    anywhere = pl.BlockSpec(memory_space=pl.ANY)
    hbm = lambda x: pltpu.with_memory_space_constraint(x, pltpu.HBM)
    vmem = pl.BlockSpec(memory_space=pltpu.VMEM)

    swap = lambda x: lax.ppermute(x, "seq", [(i, i ^ 1) for i in range(n)])
    jump = lambda x, k: lax.ppermute(x, "seq", [(i, i ^ (2 * k)) for i in range(n)])
    cross = lambda x, ks: lax.ppermute(x, "seq", [(i, i ^ (2 * ks[i % 2])) for i in range(n)])
    edges = [(i, i + 1) for i in range(1, n - 1, 2)]

    partner = swap(tokens)
    halo = lax.ppermute(tokens, "seq", edges + [(j, i) for i, j in edges])

    own = jnp.stack([w_up, w_down])
    gathered = [own]

    def gather_part(s, *earlier):
        if s < parts:
            gathered.append(lax.ppermute(after(gathered[-1], *earlier), "dp", follow))

    gather_part(1)
    share = (chips // 2, 1) if chips > 1 else ()
    shared = []

    def share_part(s, *earlier):
        if share and s < parts:
            shared.append(cross(after(gathered[s], *earlier) if earlier else gathered[s], share))


    half = heads // 2
    wide = half * HS
    block = 4 * HS
    steps = wide // block
    owned = half * rank // chips
    extra = max(16, 4 * owned // 128)
    hbm_space = pl.BlockSpec(memory_space=pltpu.HBM)
    out = call(
        functools.partial(project_kernel, (chips, owned, extra, rank)),
        [hbm_space, vmem, hbm_space, hbm_space],
        [vmem] * 6 + [anywhere] * chips,
        [shape((2 * rows, wide))] * 3
        + [shape((width, wide))] * 2
        + [shape((8, 128), F32)]
        + [shape((owned + extra, 128))] * chips,
        [
            pltpu.VMEM((rows, width), BF),
            pltpu.VMEM((width, wide), BF),
            pltpu.VMEM((half, HS, rank), BF),
            pltpu.VMEM((2 * rows, width), BF),
            pltpu.VMEM((2 * rows, wide), BF),
            pltpu.VMEM((2 * rows, wide), BF),
            pltpu.VMEM((chips, owned + extra, 128), BF),
            pltpu.VMEM((chips, extra, 128), F32),
            pltpu.SemaphoreType.DMA((5,)),
            pltpu.SemaphoreType.DMA((chips,)),
        ],
        (4 * rows * width * 3 * wide, 6 * width * wide, half * rank * 2 * rows),
    )(hbm(tokens), partner, hbm(w_qkv), hbm(w_proj))
    query, near_keys, near_values, w_key, w_value, top = out[:6]
    out = out[6:]
    pays = [out[0]]
    for k in range(1, chips):
        pays.append(jump(out[k], k))

    gather_part(2, top)
    share_part(0, top)
    near = call(
        near_kernel,
        [vmem] * 4,
        [vmem] * 2,
        [shape((2 * rows, 2 * wide), F32), shape((2 * rows, 128), F32)],
        (),
        (8 * rows * wide * 4 * rows, 8 * rows * wide, half * 2 * rows * 2 * rows),
    )(top, query, near_keys, near_values)
    pays = [after(p, near[0]) for p in pays]
    far = pl.pallas_call(
        functools.partial(combine_kernel, (chips, owned, extra)),
        out_shape=shape((owned, 128)),
        compiler_params=pltpu.CompilerParams(vmem_limit_bytes=VMEM_LIMIT),
        cost_estimate=pl.CostEstimate(flops=1000000, bytes_accessed=1000000, transcendentals=0),
    )(*pays)
    share_part(1, far)
    fars = [far]
    for k in range(1, chips):
        fars.append(jump(far, k))
    halo = after(halo, far)
    halo_partner = swap(halo)
    near = call(
        halo_kernel,
        [vmem] * 8,
        [vmem] * 2,
        [shape((2 * rows, 2 * wide), F32), shape((2 * rows, 128), F32)],
        [
            pltpu.VMEM((2 * rows, width), BF),
            pltpu.VMEM((2 * rows, wide), BF),
            pltpu.VMEM((2 * rows, wide), BF),
        ],
        (4 * rows * width * 2 * wide, 4 * width * wide, half * rows * 2 * rows),
    )(top, query, *near, halo, halo_partner, w_key, w_value)
    share_part(2, near[0])
    for s in range(3, parts):
        gather_part(s, near[0])
    fars = [after(x, near[0]) for x in fars]
    pieces = []
    for g in range(steps):
        pieces.append(
            call(
                functools.partial(far_kernel, (chips, owned, rank, g)),
                [vmem] * (4 + chips),
                [vmem] * 2,
                [shape((rows, block))] * 2,
                [pltpu.VMEM((half * rank, 128), BF)],
                (4 * rows * block * rank * 2, 6 * rows * block, 4 * rank * 2 * rows),
            )(top, query, *near, *fars)
        )
    arrived = []
    for g in range(steps):
        arrived.append(swap(pieces[g][1]))
    theirs = pieces[-1][1]
    mixed, yn, *yn_cuts = call(
        functools.partial(mix_kernel, CUTS),
        [vmem] * (2 + 2 * steps),
        [vmem] * (2 + CUTS),
        [shape((rows, width))] * 2 + [shape((rows // CUTS, width))] * CUTS,
        (),
        (4 * rows * width * wide, 2 * width * width, 0),
    )(tokens, *[piece[0] for piece in pieces], *arrived, w_out)
    for s in range(3, parts):
        share_part(s, yn)
    own_sides = list(gathered)
    for w in gathered:
        own_sides.append(swap(after(w, theirs)))

    def feed(x, dtype, weights, *more):
        return call(
            functools.partial(feed_kernel, parts, len(more)),
            [vmem] * (1 + len(weights) + len(more)),
            vmem,
            shape(x.shape, dtype),
            (),
            (2 * x.size * len(weights) * w_up.shape[1], len(weights) * own.size, rows * w_up.shape[1]),
        )(x, *weights, *more)

    routes = list(zip(*[[k for k in range(1, chips) if not k & bit] for bit in share]))
    visitors = []
    for cut in yn_cuts:
        for ks in routes:
            for which, route in enumerate((ks, ks[::-1])):
                visitors.append((which, route, cross(cut, route)))
    total = feed(yn, F32, own_sides, mixed)
    mine_sides, their_sides = list(gathered), own_sides[parts:]
    if share:
        swapped = []
        for i, w in enumerate(shared):
            swapped.append(swap(after(w, theirs if i < 2 else total)))
        mine_sides += shared
        their_sides = their_sides + swapped
    returned, last = [], total
    for which, route, x in visitors:
        last = feed(after(x, last), BF, (mine_sides, their_sides)[which])
        returned.append(cross(last, route).astype(F32))
    if share:
        total = feed(after(yn, last), F32, mine_sides[parts:] + their_sides[parts:], total)
    if returned:
        each = len(returned) // CUTS
        total = total + jnp.concatenate(
            [sum(returned[i * each : (i + 1) * each]) for i in range(CUTS)], axis=0
        )
    return total.astype(BF)[None]


def solution(mesh):
    in_specs = (P("dp", "seq", None), P(), P(), P(), P("dp", "seq"), P("dp", "seq"))
    out_specs = P("dp", "seq", None)
    return jax.shard_map(
        on_device, mesh=mesh, in_specs=in_specs, out_specs=out_specs, check_vma=False
    )
```

```python
import functools

import jax
import jax.numpy as jnp
from jax import lax
from jax.experimental import pallas as pl
from jax.experimental.pallas import tpu as pltpu
from jax.sharding import PartitionSpec as P


HS = 64
EPS = 1e-05
F32 = jnp.float32
BF = jnp.bfloat16
NT = (((1,), (1,)), ((), ()))
TT = (((0,), (1,)), ((), ()))
VMEM_LIMIT = 24 * 1024 * 1024
SMALL = 60.0
CUTS = 2
BOTH = [(side, part) for side in range(2) for part in range(2)]


def dot(a, b):
    return jnp.dot(a, b, preferred_element_type=F32)


def layer_norm(x):
    center = x - jnp.mean(x, axis=-1, keepdims=True)
    spread = jnp.mean(center * center, axis=-1, keepdims=True)
    return center * lax.rsqrt(spread + EPS)


def head_average(width):
    a = lax.broadcasted_iota(jnp.int32, (width, width), 0) // HS
    b = lax.broadcasted_iota(jnp.int32, (width, width), 1) // HS
    return jnp.where(a == b, 1.0 / HS, 0.0).astype(F32)


def split(x):
    high = x.astype(BF)
    return high, (x - high.astype(F32)).astype(BF)


def blocks_of(x, size=256):
    return [x[:, i : i + size] for i in range(0, x.shape[1], size)]


def join(parts):
    return parts[0] if len(parts) == 1 else jnp.concatenate(parts, axis=1)


def head_norm(x):
    out, top = [], []
    for y in blocks_of(x):
        avg = head_average(y.shape[1]).astype(BF)
        mean = dot(y, avg)
        center = y.astype(F32) - mean
        spread = dot((center * center).astype(BF), avg)
        out.append((center * lax.rsqrt(spread + EPS)).astype(BF))
        top.append(spread + mean * mean)
    return join(out), functools.reduce(jnp.maximum, top)


def head_sum(x):
    out = []
    for y in blocks_of(x):
        square = y.astype(F32) * y.astype(F32)
        out.append(dot(square.astype(BF), head_average(y.shape[1]).astype(BF)) * HS)
    return functools.reduce(jnp.maximum, out)


def head_norm_wide(x):
    avg = head_average(x.shape[1]).astype(BF)

    def mean(y):
        one = y.astype(BF)
        rest = y - one.astype(F32)
        two, three = split(rest)
        return dot(one, avg) + dot(two, avg) + dot(three, avg)

    center = x - mean(x)
    spread = mean(center * center)
    return (center * lax.rsqrt(spread + EPS)).astype(BF)


def lanes(shape):
    return lax.broadcasted_iota(jnp.int32, shape, len(shape) - 1)


def diagonal(size):
    return lax.broadcasted_iota(jnp.int32, (size, size), 0) == lax.broadcasted_iota(
        jnp.int32, (size, size), 1
    )


def to_row(column):
    size = column.shape[0]
    return jnp.sum(jnp.where(diagonal(size), column, 0.0), axis=0, keepdims=True)


def to_column(row):
    size = row.shape[1]
    return jnp.sum(jnp.where(diagonal(size), row, 0.0), axis=1, keepdims=True)


def place_in_seq():
    me = lax.axis_index("seq")
    return lax.rem(me, 2), lax.div(me, 2)


def project_kernel(sizes, tok_hbm, par_ref, w_hbm, wp_hbm, q_ref, nk_ref, nv_ref, wk_ref, wv_ref, top_ref, *rest):
    chips, owned, _, rank = sizes
    pays, (tok_ref, wq_ref, wp_ref, xn_ref, kk_ref, vv_ref, pay_ref, stat_ref, sem, out_sem) = rest[:chips], rest[chips:]
    rows, width = tok_ref.shape
    wide = q_ref.shape[1]
    heads = wide // HS
    core, chip = place_in_seq()
    mine = lambda which: w_hbm.at[:, pl.ds(pl.multiple_of(which * width + core * wide, wide), wide)]
    loads = [
        pltpu.make_async_copy(tok_hbm, tok_ref, sem.at[0]),
        pltpu.make_async_copy(mine(1), wk_ref, sem.at[1]),
        pltpu.make_async_copy(mine(2), wv_ref, sem.at[2]),
        pltpu.make_async_copy(wp_hbm.at[pl.ds(core * heads, heads)], wp_ref, sem.at[3]),
        pltpu.make_async_copy(mine(0), wq_ref, sem.at[4]),
    ]
    for load in loads:
        load.start()
    xn_ref[rows:] = layer_norm(par_ref[...].astype(F32)).astype(BF)
    stat_ref[...] = jnp.zeros_like(stat_ref)
    loads[0].wait()
    xn_ref[:rows] = layer_norm(tok_ref[...].astype(F32)).astype(BF)
    x = xn_ref[...]
    loads[1].wait()
    kk = dot(x, wk_ref[...]).astype(BF)
    kk_ref[...] = kk
    loads[2].wait()
    vv = dot(x, wv_ref[...]).astype(BF)
    vv_ref[...] = vv
    loads[3].wait()
    nk_ref[...], key_top = head_norm(kk)
    nv_ref[...], _ = head_norm(vv)
    loads[4].wait()
    query = (dot(x, wq_ref[...]).astype(BF).astype(F32) * HS ** (-0.5)).astype(BF)
    q_ref[...] = query
    top_ref[...] = jnp.broadcast_to(jnp.max(head_sum(query)), top_ref.shape)
    stat_rows = owned // 128

    def score(pair, side):
        wp = wp_ref[pair * 2 + side]
        none = jnp.zeros_like(wp)
        wide_wp = jnp.concatenate([wp, none] if side == 0 else [none, wp], axis=0)
        return lax.dot_general(wide_wp, kk_ref[:, pair_cut(pair)], TT, preferred_element_type=F32)

    def finish(pair, side, logits, shifted):
        kp, vp = kk_ref[:, pair_cut(pair)], vv_ref[:, pair_cut(pair)]
        turned = pltpu.roll(vp.astype(F32), 64, 1).astype(BF)
        low_half = lanes(kp.shape) < HS
        mixed = jnp.where(low_half, kp, turned) if side == 0 else jnp.where(low_half, turned, kp)
        if shifted:
            peak = jnp.max(logits, axis=1, keepdims=True)
            logits = logits - peak
        weight = jnp.exp(logits).astype(BF)
        total = jnp.sum(weight.astype(F32), axis=1, keepdims=True)
        sums = dot(weight, mixed).astype(BF)
        for part in range(rank // 128):
            column = (pair * 2 + side) * rank + part * 128
            owner, offset = column // owned, column % owned
            here = slice(part * 128, (part + 1) * 128)
            pay_ref[owner, pl.ds(pl.multiple_of(offset, 128), 128), :] = sums[here]
            entries = [(3, to_row(total[here]))]
            if shifted:
                one = to_row(peak[here])
                first = one.astype(BF).astype(F32)
                second = (one - first).astype(BF).astype(F32)
                entries += [(0, first), (1, second), (2, one - first - second)]
            for i, row in entries:
                stat_ref[owner, pl.ds(i * stat_rows + offset // 128, 1), :] = row

    column_norm = jnp.max(jnp.sum(jnp.square(wp_ref[...].astype(F32)), axis=1))
    near_zero = jnp.max(key_top) * HS * column_norm < SMALL * SMALL

    one_ahead(near_zero, heads // 2, [(0,), (1,)], score, finish)
    pay_ref[:, owned:, :] = stat_ref[...].astype(BF)
    copies = [
        pltpu.make_async_copy(pay_ref.at[lax.bitwise_xor(chip, k)], pays[k], out_sem.at[k]) for k in range(chips)
    ]
    for copy in copies:
        copy.start()
    for copy in copies:
        copy.wait()


def combine_kernel(sizes, *refs):
    chips, owned, extra = sizes
    pays, far_ref = refs[:chips], refs[chips]
    stat_rows = owned // 128
    tails = [p[owned : owned + extra, :].astype(F32) for p in pays]
    peaks = [
        t[:stat_rows] + t[stat_rows : 2 * stat_rows] + t[2 * stat_rows : 3 * stat_rows] for t in tails
    ]
    peak = functools.reduce(jnp.maximum, peaks)
    scales = [jnp.exp(p - peak) for p in peaks]
    total = sum(s * t[3 * stat_rows : 4 * stat_rows] for s, t in zip(scales, tails))
    scales = [s / total for s in scales]
    for i in range(stat_rows):
        cut = slice(i * 128, (i + 1) * 128)
        summary = sum(to_column(s[i : i + 1]) * p[cut, :].astype(F32) for s, p in zip(scales, pays))
        far_ref[cut, :] = head_norm_wide(summary)


def one_head(qp, side):
    low_half = lanes(qp.shape) < HS
    none = jnp.zeros_like(qp)
    return jnp.where(low_half, qp, none) if side == 0 else jnp.where(low_half, none, qp)


def with_ones(v, side):
    low_half = lanes(v.shape) < HS
    ones = jnp.ones_like(v)
    return jnp.where(low_half, v, ones) if side == 0 else jnp.where(low_half, ones, v)


def small_scores(top_ref):
    return jnp.max(top_ref[...]) * (HS * 1.02) < SMALL * SMALL


def one_ahead(small, pairs, kinds, score, finish):
    @pl.when(small)
    def _():
        units = [(pair, *kind) for pair in range(pairs) for kind in kinds]
        ahead = score(*units[0])
        for i, unit in enumerate(units):
            scores, ahead = ahead, score(*units[i + 1]) if i + 1 < len(units) else None
            finish(*unit, scores, False)

    @pl.when(jnp.logical_not(small))
    def _():
        def one(pair, carry):
            for kind in kinds:
                finish(pair, *kind, score(pair, *kind), True)
            return carry

        lax.fori_loop(0, pairs, one, 0)


def pair_cut(pair):
    return pl.ds(pl.multiple_of(pair * 128, 128), 128)


def near_kernel(top_ref, q_ref, nk_ref, nv_ref, o_ref, m_ref):
    rows = q_ref.shape[0] // 2
    place = lanes((rows, 128))
    m_ref[...] = jnp.zeros_like(m_ref)

    def rows_of(part):
        return slice(part * rows, (part + 1) * rows)

    def score(pair, side, part):
        qm = one_head(q_ref[rows_of(part), pair_cut(pair)], side)
        return lax.dot_general(qm, nk_ref[:, pair_cut(pair)], NT, preferred_element_type=F32)

    def finish(pair, side, part, scores, shifted):
        these = rows_of(part)
        if shifted:
            peak = jnp.max(scores, axis=1, keepdims=True)
            scores = scores - peak
            m_ref[these] = jnp.where(place == pair * 2 + side, peak, m_ref[these])
        vp = with_ones(nv_ref[:, pair_cut(pair)], side)
        o_ref[these, pair_cut(pair * 2 + side)] = dot(jnp.exp(scores).astype(BF), vp)

    one_ahead(small_scores(top_ref), nk_ref.shape[1] // 128, BOTH, score, finish)


def halo_kernel(top_ref, q_ref, before_ref, mb_ref, halo_ref, halop_ref, wk_ref, wv_ref, o_ref, m_ref, xh_ref, hk_ref, hv_ref):
    rows = halo_ref.shape[0]
    xh_ref[:rows] = layer_norm(halo_ref[...].astype(F32)).astype(BF)
    xh_ref[rows:] = layer_norm(halop_ref[...].astype(F32)).astype(BF)
    x = xh_ref[...]
    hk_ref[...], _ = head_norm(dot(x, wk_ref[...]).astype(BF))
    hv_ref[...], _ = head_norm(dot(x, wv_ref[...]).astype(BF))
    me, n = lax.axis_index("seq"), lax.axis_size("seq")
    other = lax.bitwise_xor(me, 1)
    inside = [(i > 0) & (i < n - 1) for i in (me, other)]
    place = lanes((rows, 128))
    m_ref[...] = mb_ref[...]

    def rows_of(part):
        return slice(part * rows, (part + 1) * rows)

    def score(pair, side, part):
        these, cut = rows_of(part), pair_cut(pair)
        qm = one_head(q_ref[these, cut], side)
        scores = lax.dot_general(qm, hk_ref[these, cut], NT, preferred_element_type=F32)
        return scores + jnp.where(inside[part], 0.0, -jnp.inf).astype(F32)

    def finish(pair, side, part, scores, shifted):
        these, here = rows_of(part), pair_cut(pair * 2 + side)
        before = before_ref[these, here]
        if shifted:
            head = place == pair * 2 + side
            peak = jnp.sum(jnp.where(head, mb_ref[these], 0.0), axis=1, keepdims=True)
            new = jnp.maximum(peak, jnp.max(scores, axis=1, keepdims=True))
            scores = scores - new
            before = before * jnp.exp(peak - new)
            m_ref[these] = jnp.where(head, new, m_ref[these])
        values = with_ones(hv_ref[these, pair_cut(pair)], side)
        o_ref[these, here] = before + dot(jnp.exp(scores).astype(BF), values)

    one_ahead(small_scores(top_ref), hk_ref.shape[1] // 128, BOTH, score, finish)


def far_kernel(sizes, top_ref, q_ref, o_ref, m_ref, *rest):
    chips, owned, rank, group = sizes
    fars, (mine_ref, theirs_ref, all_ref) = rest[:chips], rest[chips:]
    rows = mine_ref.shape[0]
    heads = mine_ref.shape[1] // HS
    _, chip = place_in_seq()
    for k in range(chips):
        source = lax.bitwise_xor(chip, k)
        all_ref[pl.ds(pl.multiple_of(source * owned, owned), owned), :] = fars[k][...]
    place = lanes((rows, 128))

    def rows_of(part):
        return slice(part * rows, (part + 1) * rows)

    def pair_of(pair):
        return group * (heads // 2) + pair

    def summary(pair, side):
        head = pair_of(pair) * 2 + side
        return all_ref[pl.ds(pl.multiple_of(head * rank, rank), rank), :]

    def score(pair, part):
        query = q_ref[rows_of(part), pair_cut(pair_of(pair))]
        return [
            lax.dot_general(one_head(query, side), summary(pair, side), NT, preferred_element_type=F32)
            for side in range(2)
        ]

    def finish(pair, part, scores, shifted):
        these = rows_of(part)
        low_half = lanes((rows, 128)) < HS
        sums = []
        for side in range(2):
            head = pair_of(pair) * 2 + side
            weight = scores[side]
            before = o_ref[these, pair_cut(head)]
            if shifted:
                peak = jnp.sum(jnp.where(place == head, m_ref[these], 0.0), axis=1, keepdims=True)
                new = jnp.maximum(peak, jnp.max(weight, axis=1, keepdims=True))
                weight = weight - new
                before = before * jnp.exp(peak - new)
            out = dot(jnp.exp(weight).astype(BF), with_ones(summary(pair, side), 1 - side))
            sums.append(before + pltpu.roll(out, 64, 1))
        total = pltpu.roll(jnp.where(low_half, sums[1], sums[0]), 64, 1)
        result = (jnp.where(low_half, sums[0], sums[1]) / total).astype(BF)
        (mine_ref, theirs_ref)[part][:, pair_cut(pair)] = result

    one_ahead(small_scores(top_ref), heads // 2, [(0,), (1,)], score, finish)


def mix_kernel(cuts, tok_ref, *rest):
    rest, cut_refs = rest[:-cuts], rest[-cuts:]
    pieces, (w_ref, mixed_ref, yn_ref) = rest[:-3], rest[-3:]
    wide = pieces[0].shape[1]
    half = len(pieces) // 2
    total = 0.0
    core, _ = place_in_seq()
    for i, piece in enumerate(pieces):
        owner = core if i < half else 1 - core
        start = pl.multiple_of((owner * half + i % half) * wide, wide)
        total = total + dot(piece[...], w_ref[pl.ds(start, wide), :])
    mixed = (tok_ref[...].astype(F32) + total).astype(BF)
    mixed_ref[...] = mixed
    yn = layer_norm(mixed.astype(F32)).astype(BF)
    yn_ref[...] = yn
    size = yn.shape[0] // cuts
    for i, cut_ref in enumerate(cut_refs):
        cut_ref[...] = yn[i * size : (i + 1) * size]


def gelu(v):
    return 0.5 * v * (1.0 + jnp.tanh((2.0 / jnp.pi) ** 0.5 * (v + 0.044715 * (v * v * v))))


def folded(size):
    return [0] + list(range(1, size, 2)) + list(range(2, size, 2))[::-1]


def feed_kernel(parts, added, yn_ref, *rest):
    rest, more, out_ref = rest[: -1 - added], rest[-1 - added : -1], rest[-1]
    sides = len(rest) // parts
    depth = rest[0].shape[1]
    dp = lax.axis_index("dp")
    ring = folded(parts)
    starts = []
    for s in range(parts):
        block = sum(jnp.where(dp == ring[i], ring[(i - s) % parts], 0) for i in range(parts))
        starts.append(pl.multiple_of(block * depth, depth))
    hidden = []
    for side in range(sides):
        bufs = rest[side * parts : (side + 1) * parts]
        total = sum(dot(yn_ref[:, pl.ds(starts[i], depth)], bufs[i][0]) for i in range(parts))
        hidden.append(gelu(total).astype(BF))
    for i in range(parts):
        total = sum(
            lax.dot_general(hidden[side], rest[side * parts + i][1], NT, preferred_element_type=F32)
            for side in range(sides)
        )
        for ref in more:
            total = total + ref[:, pl.ds(starts[i], depth)].astype(F32)
        out_ref[:, pl.ds(starts[i], depth)] = total.astype(out_ref.dtype)


def call(kernel, in_specs, out_specs, out_shape, scratch=(), cost=(0, 0, 0)):
    return pl.pallas_call(
        kernel,
        in_specs=in_specs,
        out_specs=out_specs,
        scratch_shapes=scratch,
        out_shape=out_shape,
        compiler_params=pltpu.CompilerParams(vmem_limit_bytes=VMEM_LIMIT),
        cost_estimate=pl.CostEstimate(flops=cost[0], bytes_accessed=cost[1], transcendentals=cost[2]),
    )


def shape(dims, dtype=BF):
    return jax.ShapeDtypeStruct(dims, dtype)


def after(x, *earlier):
    return lax.optimization_barrier((x,) + earlier)[0]


def on_device(layer_input, w_qkv, w_out, w_proj, w_up, w_down):
    tokens = layer_input[0]
    rows, width = tokens.shape
    heads, _, rank = w_proj.shape
    n, parts = lax.axis_size("seq"), lax.axis_size("dp")
    chips = n // 2
    ring = folded(parts)
    follow = [(ring[i], ring[(i + 1) % parts]) for i in range(parts)]
    anywhere = pl.BlockSpec(memory_space=pl.ANY)
    hbm = lambda x: pltpu.with_memory_space_constraint(x, pltpu.HBM)
    vmem = pl.BlockSpec(memory_space=pltpu.VMEM)

    swap = lambda x: lax.ppermute(x, "seq", [(i, i ^ 1) for i in range(n)])
    jump = lambda x, k: lax.ppermute(x, "seq", [(i, i ^ (2 * k)) for i in range(n)])
    cross = lambda x, ks: lax.ppermute(x, "seq", [(i, i ^ (2 * ks[i % 2])) for i in range(n)])
    edges = [(i, i + 1) for i in range(1, n - 1, 2)]

    partner = swap(tokens)
    halo = lax.ppermute(tokens, "seq", edges + [(j, i) for i, j in edges])

    own = jnp.stack([w_up, w_down])
    gathered = [own]

    def gather_part(s, *earlier):
        if s < parts:
            gathered.append(lax.ppermute(after(gathered[-1], *earlier), "dp", follow))

    gather_part(1)
    share = (chips // 2, 1) if chips > 1 else ()
    shared = []

    def share_part(s, *earlier):
        if share and s < parts:
            shared.append(cross(after(gathered[s], *earlier) if earlier else gathered[s], share))


    half = heads // 2
    wide = half * HS
    block = 4 * HS
    steps = wide // block
    owned = half * rank // chips
    extra = max(16, 4 * owned // 128)
    hbm_space = pl.BlockSpec(memory_space=pltpu.HBM)
    out = call(
        functools.partial(project_kernel, (chips, owned, extra, rank)),
        [hbm_space, vmem, hbm_space, hbm_space],
        [vmem] * 6 + [anywhere] * chips,
        [shape((2 * rows, wide))] * 3
        + [shape((width, wide))] * 2
        + [shape((8, 128), F32)]
        + [shape((owned + extra, 128))] * chips,
        [
            pltpu.VMEM((rows, width), BF),
            pltpu.VMEM((width, wide), BF),
            pltpu.VMEM((half, HS, rank), BF),
            pltpu.VMEM((2 * rows, width), BF),
            pltpu.VMEM((2 * rows, wide), BF),
            pltpu.VMEM((2 * rows, wide), BF),
            pltpu.VMEM((chips, owned + extra, 128), BF),
            pltpu.VMEM((chips, extra, 128), F32),
            pltpu.SemaphoreType.DMA((5,)),
            pltpu.SemaphoreType.DMA((chips,)),
        ],
        (4 * rows * width * 3 * wide, 6 * width * wide, half * rank * 2 * rows),
    )(hbm(tokens), partner, hbm(w_qkv), hbm(w_proj))
    query, near_keys, near_values, w_key, w_value, top = out[:6]
    out = out[6:]
    pays = [out[0]]
    for k in range(1, chips):
        pays.append(jump(out[k], k))

    gather_part(2, top)
    share_part(0, top)
    near = call(
        near_kernel,
        [vmem] * 4,
        [vmem] * 2,
        [shape((2 * rows, 2 * wide), F32), shape((2 * rows, 128), F32)],
        (),
        (8 * rows * wide * 4 * rows, 8 * rows * wide, half * 2 * rows * 2 * rows),
    )(top, query, near_keys, near_values)
    pays = [after(p, near[0]) for p in pays]
    halo = after(halo, near[0])
    halo_partner = swap(halo)
    far = pl.pallas_call(
        functools.partial(combine_kernel, (chips, owned, extra)),
        out_shape=shape((owned, 128)),
        compiler_params=pltpu.CompilerParams(vmem_limit_bytes=VMEM_LIMIT),
        cost_estimate=pl.CostEstimate(flops=1000000, bytes_accessed=1000000, transcendentals=0),
    )(*pays)
    share_part(1, far)
    fars = [far]
    for k in range(1, chips):
        fars.append(jump(far, k))
    near = call(
        halo_kernel,
        [vmem] * 8,
        [vmem] * 2,
        [shape((2 * rows, 2 * wide), F32), shape((2 * rows, 128), F32)],
        [
            pltpu.VMEM((2 * rows, width), BF),
            pltpu.VMEM((2 * rows, wide), BF),
            pltpu.VMEM((2 * rows, wide), BF),
        ],
        (4 * rows * width * 2 * wide, 4 * width * wide, half * rows * 2 * rows),
    )(top, query, *near, halo, halo_partner, w_key, w_value)
    share_part(2, near[0])
    for s in range(3, parts):
        gather_part(s, near[0])
    fars = [after(x, near[0]) for x in fars]
    pieces = []
    for g in range(steps):
        pieces.append(
            call(
                functools.partial(far_kernel, (chips, owned, rank, g)),
                [vmem] * (4 + chips),
                [vmem] * 2,
                [shape((rows, block))] * 2,
                [pltpu.VMEM((half * rank, 128), BF)],
                (4 * rows * block * rank * 2, 6 * rows * block, 4 * rank * 2 * rows),
            )(top, query, *near, *fars)
        )
    arrived = []
    for g in range(steps):
        arrived.append(swap(pieces[g][1]))
    theirs = pieces[-1][1]
    mixed, yn, *yn_cuts = call(
        functools.partial(mix_kernel, CUTS),
        [vmem] * (2 + 2 * steps),
        [vmem] * (2 + CUTS),
        [shape((rows, width))] * 2 + [shape((rows // CUTS, width))] * CUTS,
        (),
        (4 * rows * width * wide, 2 * width * width, 0),
    )(tokens, *[piece[0] for piece in pieces], *arrived, w_out)
    for s in range(3, parts):
        share_part(s, yn)
    own_sides = list(gathered)
    for w in gathered:
        own_sides.append(swap(after(w, theirs)))

    def feed(x, dtype, weights, *more):
        return call(
            functools.partial(feed_kernel, parts, len(more)),
            [vmem] * (1 + len(weights) + len(more)),
            vmem,
            shape(x.shape, dtype),
            (),
            (2 * x.size * len(weights) * w_up.shape[1], len(weights) * own.size, rows * w_up.shape[1]),
        )(x, *weights, *more)

    routes = list(zip(*[[k for k in range(1, chips) if not k & bit] for bit in share]))
    visitors = []
    for cut in yn_cuts:
        for ks in routes:
            for which, route in enumerate((ks, ks[::-1])):
                visitors.append((which, route, cross(cut, route)))
    total = feed(yn, F32, own_sides, mixed)
    mine_sides, their_sides = list(gathered), own_sides[parts:]
    if share:
        swapped = []
        for i, w in enumerate(shared):
            swapped.append(swap(after(w, theirs if i < 2 else total)))
        mine_sides += shared
        their_sides = their_sides + swapped
    returned, last = [], total
    for which, route, x in visitors:
        last = feed(after(x, last), BF, (mine_sides, their_sides)[which])
        returned.append(cross(last, route).astype(F32))
    if share:
        total = feed(after(yn, last), F32, mine_sides[parts:] + their_sides[parts:], total)
    if returned:
        each = len(returned) // CUTS
        total = total + jnp.concatenate(
            [sum(returned[i * each : (i + 1) * each]) for i in range(CUTS)], axis=0
        )
    return total.astype(BF)[None]


def solution(mesh):
    in_specs = (P("dp", "seq", None), P(), P(), P(), P("dp", "seq"), P("dp", "seq"))
    out_specs = P("dp", "seq", None)
    return jax.shard_map(
        on_device, mesh=mesh, in_specs=in_specs, out_specs=out_specs, check_vma=False
    )
```
